32 devices in a mesh: snap: 8 (over z, x), feat: 4 (over y, core).
Axes of the slice: x: 2, y: 2, z: 4, core: 2. Of those that a mesh axis runs over, the one named last changes fastest.
Arguments:
- node_features: bfloat16 [16, 512, 256], P('snap', None, 'feat'), may hold values from -6 to 6
- tile_rows: int32 [16, 8], P('snap'), may hold values from 0 to 3
- tile_cols: int32 [16, 8], P('snap'), may hold values from 0 to 3, as said below
- tile_counts: int32 [16], P('snap'), may hold values from 4 to 8, as said below
- tile_values: bfloat16 [16, 8, 128, 128], P('snap'), may hold values from -0.5 to 0.5
- layer_one: bfloat16 [256, 256], replicated, may hold values from -0.375 to 0.375
- layer_two: bfloat16 [256, 256], replicated, may hold values from -0.375 to 0.375
- query_weight: bfloat16 [256, 256], replicated, may hold values from -1.25 to 1.25
- key_weight: bfloat16 [256, 256], replicated, may hold values from -1.25 to 1.25
- value_weight: bfloat16 [256, 256], replicated, may hold values from -0.375 to 0.375
- out_weight: bfloat16 [256, 256], replicated, may hold values from -0.375 to 0.375
Outputs:
- evolved: bfloat16 [16, 512, 256], P('snap', None, 'feat')
The draws below stay inside these ranges and needn't reach their ends.
Inputs may be any that keep to these rules, and one draw needn't show every extreme that they name: `tile_cols`: block columns of the tile slots; a coordinate pair may be listed more than once, and such tiles add. `tile_counts`: some snapshot uses all 8 slots.
All inputs are finite; a program needn't handle non-finite values.
Results may differ from the reference program's by a relative error of at most 0.02.
The reference program's roundings to bfloat16 on the way count: a program that leaves them out, or rounds other values in their place, can miss the bound.
Values may be sent and summed in bfloat16 or wider, within the bound.
A program may use at most 64 MiB of HBM per device.

```python
import jax
import jax.numpy as jnp
from jax import lax

D = 256
HEADS = 8
TILE = 128
HEAD_DIM = 32
SNAPS = 16
VERT = 512
BLOCKS = 4
MAXT = 8
N_SNAP = 8


def tile_lists(key):
    row_ids = jax.random.randint(jax.random.fold_in(key, 101), (SNAPS, MAXT), 0, BLOCKS)
    col_ids = jax.random.randint(jax.random.fold_in(key, 102), (SNAPS, MAXT), 0, BLOCKS)
    levels = jax.random.randint(jax.random.fold_in(key, 103), (SNAPS,), 0, 11)
    counts = 4 + (MAXT - 4) * levels * levels * levels // 1000
    full_snapshot = jax.random.randint(jax.random.fold_in(key, 104), (), 0, SNAPS)
    counts = jnp.where(jnp.arange(SNAPS) == full_snapshot, MAXT, counts)
    return (row_ids.astype(jnp.int32), col_ids.astype(jnp.int32), counts.astype(jnp.int32))


def draw_tile_rows(key, part):
    return tile_lists(key)[0]


def draw_tile_cols(key, part):
    return tile_lists(key)[1]


def draw_tile_counts(key, part):
    return tile_lists(key)[2]


def attention_pair(key, which):
    separate = jnp.clip(jax.random.normal(jax.random.fold_in(key, 202 + which), (D, D), jnp.float32), -5.0, 5.0)
    combined = separate
    return (combined * D ** (-0.5)).astype(jnp.bfloat16)


def draw_query_weight(key, part):
    return attention_pair(key, 0)


def draw_key_weight(key, part):
    return attention_pair(key, 1)


def block_scale(rng, dims, split, smallest, largest):
    loudness = 1.0
    for axis_at, shards_of in split:
        draws = jax.random.uniform(jax.random.fold_in(jax.random.fold_in(rng, 6), axis_at), (shards_of,), jnp.float32, smallest / len(split), largest / len(split))
        loudness = loudness * jnp.repeat(jnp.exp(draws), dims[axis_at] // shards_of).reshape((-1,) + (1,) * (len(dims) - 1 - axis_at))
    return loudness


def normal_values(key, extent, spread, limit, split=(), kind=jnp.bfloat16):
    array = spread * jax.random.normal(key, extent, jnp.float32)
    if split:
        array = array * block_scale(key, extent, split, -0.22, 0.18)
    return jnp.clip(array, -limit, limit).astype(kind)


def setup_inputs(seed: int = 0) -> dict:
    splits = jax.random.split(jax.random.key(seed), 12)
    return {
        "node_features": normal_values(splits[0], (SNAPS, VERT, D), 1.0, 6.0, ((0, 8), (2, 4))),
        "tile_rows": draw_tile_rows(jax.random.fold_in(splits[11], 71), 0),
        "tile_cols": draw_tile_cols(jax.random.fold_in(splits[11], 71), 0),
        "tile_counts": draw_tile_counts(jax.random.fold_in(splits[11], 71), 0),
        "tile_values": normal_values(splits[4], (SNAPS, MAXT, TILE, TILE), TILE ** -0.5, 0.5, ((0, 8),)),
        "layer_one": normal_values(splits[5], (D, D), D ** -0.5, 0.375),
        "layer_two": normal_values(splits[6], (D, D), D ** -0.5, 0.375),
        "query_weight": draw_query_weight(jax.random.fold_in(splits[11], 71), 0),
        "key_weight": draw_key_weight(jax.random.fold_in(splits[11], 71), 0),
        "value_weight": normal_values(splits[9], (D, D), D ** -0.5, 0.375),
        "out_weight": normal_values(splits[10], (D, D), D ** -0.5, 0.375),
    }


masked_score = -1.0e30


def spread_snapshot(features, tile_block, block_rows, block_cols, slot_count):
    feat_width = features.shape[1]
    blocked = features.reshape(BLOCKS, TILE, feat_width)
    picked_blocks = blocked[block_cols]
    live_slots = (jnp.arange(MAXT, dtype=jnp.int32) < slot_count)
    products = jnp.einsum("irc,icf->irf", tile_block.astype(jnp.float32), picked_blocks.astype(jnp.float32), precision=lax.Precision.HIGHEST)
    products = products * live_slots.astype(jnp.float32)[:, None, None]
    membership = ((block_rows[None, :] == jnp.arange(BLOCKS, dtype=jnp.int32)[:, None]) & live_slots[None, :]).astype(jnp.float32)
    summed = jnp.dot(membership, products.reshape(MAXT, TILE * feat_width), precision=lax.Precision.HIGHEST)
    return summed.reshape(VERT, feat_width).astype(jnp.bfloat16)


def attend_block(hidden, query_weight, key_weight, value_weight, out_weight):
    snaps, verts, model_width = hidden.shape
    flat = hidden.reshape(snaps * verts, model_width)

    def project(weight):
        return jnp.dot(flat, weight, preferred_element_type=jnp.float32).astype(jnp.bfloat16).reshape(snaps, verts, HEADS, HEAD_DIM)

    query_heads = project(query_weight)
    key_heads = project(key_weight)
    value_heads = project(value_weight)
    scores = jnp.einsum("tvhd,uvhd->vhtu", query_heads.astype(jnp.float32), key_heads.astype(jnp.float32)) * (HEAD_DIM ** -0.5)
    causal = jnp.arange(snaps, dtype=jnp.int32)[:, None] >= jnp.arange(snaps, dtype=jnp.int32)[None, :]
    scores = jnp.where(causal, scores, masked_score)
    row_max = jnp.max(scores, axis=-1, keepdims=True)
    lifted = jnp.exp(scores - row_max)
    weights = (lifted / jnp.sum(lifted, axis=-1, keepdims=True)).astype(jnp.bfloat16)
    context = jnp.einsum("vhtu,uvhd->tvhd", weights.astype(jnp.float32), value_heads.astype(jnp.float32)).astype(jnp.bfloat16)
    context = context.reshape(snaps * verts, model_width)
    result = flat.astype(jnp.float32) + jnp.dot(context, out_weight, preferred_element_type=jnp.float32)
    return result.astype(jnp.bfloat16).reshape(snaps, verts, model_width)


def reference(node_features, tile_rows, tile_cols, tile_counts, tile_values, layer_one, layer_two, query_weight, key_weight, value_weight, out_weight):
    def evolve_snapshot(packed):
        features, tile_block, block_rows, block_cols, slot_count = packed
        spread_one = spread_snapshot(features, tile_block, block_rows, block_cols, slot_count)
        mixed_one = jnp.dot(spread_one, layer_one, preferred_element_type=jnp.float32)
        hidden_one = (features.astype(jnp.float32) + jnp.maximum(mixed_one, 0.0)).astype(jnp.bfloat16)
        spread_two = spread_snapshot(hidden_one, tile_block, block_rows, block_cols, slot_count)
        mixed_two = jnp.dot(spread_two, layer_two, preferred_element_type=jnp.float32)
        return (hidden_one.astype(jnp.float32) + jnp.maximum(mixed_two, 0.0)).astype(jnp.bfloat16)

    hidden_two = lax.map(evolve_snapshot, (node_features, tile_values, tile_rows, tile_cols, tile_counts))
    vert_block = VERT // N_SNAP
    grouped = hidden_two.reshape(SNAPS, N_SNAP, vert_block, D).transpose(1, 0, 2, 3)

    def attend_group(hidden):
        return attend_block(hidden, query_weight, key_weight, value_weight, out_weight)

    attended = lax.map(attend_group, grouped)
    return attended.transpose(1, 0, 2, 3).reshape(SNAPS, VERT, D)
```

```python
import functools
import math

import jax
import jax.numpy as jnp
from jax import lax
from jax.experimental import pallas as pl
from jax.experimental.pallas import tpu as pltpu
from jax.sharding import PartitionSpec as P

HEADS = 8


masked_score = -1e30


def spread_padded(features, tile_block, block_rows, block_cols, slot_count):
    vert_count, feat_width = features.shape
    tile_side = tile_block.shape[1]
    slot_total = tile_block.shape[0]
    block_count = vert_count // tile_side
    blocked = features.reshape(block_count, tile_side, feat_width)
    picked_blocks = blocked[block_cols]
    live_slots = jnp.arange(slot_total, dtype=jnp.int32) < slot_count
    products = jnp.einsum(
        "irc,icf->irf", tile_block, picked_blocks, preferred_element_type=jnp.float32
    )
    products = products * live_slots.astype(jnp.float32)[:, None, None]
    membership = (
        (block_rows[None, :] == jnp.arange(block_count, dtype=jnp.int32)[:, None])
        & live_slots[None, :]
    ).astype(jnp.float32)
    summed = jnp.dot(
        membership,
        products.reshape(slot_total, tile_side * feat_width),
        precision=lax.Precision.HIGHEST,
    )
    return summed.reshape(vert_count, feat_width).astype(jnp.bfloat16)


def attend_local(hidden, query_weight, key_weight, value_weight, out_weight):
    snaps, verts, model_width = hidden.shape
    head_dim = model_width // HEADS
    flat = hidden.reshape(snaps * verts, model_width)

    def project(weight):
        return (
            jnp.dot(flat, weight, preferred_element_type=jnp.float32)
            .astype(jnp.bfloat16)
            .reshape(snaps, verts, HEADS, head_dim)
        )

    query_heads = project(query_weight)
    key_heads = project(key_weight)
    value_heads = project(value_weight)
    scores = jnp.einsum(
        "tvhd,uvhd->vhtu", query_heads, key_heads, preferred_element_type=jnp.float32
    ) * head_dim ** (-0.5)
    causal = (
        jnp.arange(snaps, dtype=jnp.int32)[:, None] >= jnp.arange(snaps, dtype=jnp.int32)[None, :]
    )
    scores = jnp.where(causal, scores, masked_score)
    row_max = jnp.max(scores, axis=-1, keepdims=True)
    lifted = jnp.exp(scores - row_max)
    weights = (lifted / jnp.sum(lifted, axis=-1, keepdims=True)).astype(jnp.bfloat16)
    context = jnp.einsum(
        "vhtu,uvhd->tvhd", weights, value_heads, preferred_element_type=jnp.float32
    ).astype(jnp.bfloat16)
    context = context.reshape(snaps * verts, model_width)
    result = flat.astype(jnp.float32) + jnp.dot(
        context, out_weight, preferred_element_type=jnp.float32
    )
    return result.astype(jnp.bfloat16).reshape(snaps, verts, model_width)


def on_device(
    node_features,
    tile_rows,
    tile_cols,
    tile_counts,
    tile_values,
    layer_one,
    layer_two,
    query_weight,
    key_weight,
    value_weight,
    out_weight,
):
    snap_dev, vert_count, feat_width = node_features.shape
    feat_index = lax.axis_index("feat")

    def spread_all(features):
        spread_pieces = []
        for snapshot in range(snap_dev):
            spread_pieces.append(
                spread_padded(
                    features[snapshot],
                    tile_values[snapshot],
                    tile_rows[snapshot],
                    tile_cols[snapshot],
                    tile_counts[snapshot],
                )
            )
        return jnp.stack(spread_pieces, axis=0)

    def convolve(features, weight):
        spread_rows = spread_all(features).reshape(snap_dev * vert_count, feat_width)
        own_columns = lax.dynamic_slice_in_dim(weight, feat_index * feat_width, feat_width, 1)
        mixed_sum = jnp.dot(
            lax.all_gather(spread_rows, "feat", axis=1, tiled=True),
            own_columns,
            preferred_element_type=jnp.float32,
        )
        mixed_sum = mixed_sum.reshape(snap_dev, vert_count, feat_width)
        return (features.astype(jnp.float32) + jnp.maximum(mixed_sum, 0.0)).astype(jnp.bfloat16)

    hidden_one = convolve(node_features, layer_one)
    hidden_two = convolve(hidden_one, layer_two)
    vertex_rows = lax.all_to_all(
        lax.all_to_all(hidden_two, "snap", split_axis=1, concat_axis=0, tiled=True),
        "feat",
        split_axis=1,
        concat_axis=2,
        tiled=True,
    )
    attended = attend_local(vertex_rows, query_weight, key_weight, value_weight, out_weight)
    return lax.all_to_all(
        lax.all_to_all(attended, "feat", split_axis=2, concat_axis=1, tiled=True),
        "snap",
        split_axis=0,
        concat_axis=1,
        tiled=True,
    )


LANES = 128
SUBLANES = 8
MESH = pl.DeviceIdType.MESH


def fused_kernel(
    n_snap,
    n_feat,
    rows_ref,
    cols_ref,
    counts_ref,
    feat_ref,
    tiles_ref,
    w_one,
    w_two,
    w_query,
    w_key,
    w_value,
    w_out,
    out_ref,
    tiles,
    weights,
    pieces,
    adjacency,
    features,
    hidden_one,
    hidden_two,
    vertex_rows,
    outgoing,
    returned,
    load_sem,
    gather_send,
    gather_recv,
    spread_send,
    spread_recv,
    return_send,
    return_recv,
):
    snap_dev, feat_width, vert_count = feat_ref.shape
    slot_total, tile_side, _ = tiles.shape
    block_count = vert_count // tile_side
    snaps, vert_dev, width = vertex_rows.shape
    parts = n_feat // snap_dev
    part_rows = vert_count // parts
    total = n_snap * n_feat
    head_dim = width // HEADS

    me_snap = lax.axis_index("snap")
    me_feat = lax.axis_index("feat")
    me = me_snap * n_feat + me_feat
    part = me_feat % parts
    local = me_feat // parts
    own = me_snap * snap_dev + local

    def load(source, target, at):
        copy = pltpu.make_async_copy(source, target, load_sem.at[at])
        copy.start()
        return copy

    tile_load = load(tiles_ref.at[local], tiles, 1)
    weight_loads = [
        load(ref, weights.at[at], 2 + at)
        for at, ref in enumerate((w_one, w_two, w_query, w_key, w_value, w_out))
    ]

    barrier = pltpu.get_barrier_semaphore()
    for step in range(1, total):
        peer = (me + step) % total
        pl.semaphore_signal(
            barrier, inc=1, device_id=(peer // n_feat, peer % n_feat), device_id_type=MESH
        )

    pl.semaphore_wait(barrier, total - 1)

    gathers = []
    for step in [n_feat // 2] + [s for s in range(1, n_feat) if s != n_feat // 2]:
        peer = (me_feat + step) % n_feat
        copy = pltpu.make_async_remote_copy(
            src_ref=feat_ref.at[peer // parts],
            dst_ref=pieces.at[me_feat],
            send_sem=gather_send.at[step],
            recv_sem=gather_recv.at[step],
            device_id=(me_snap, peer),
            device_id_type=MESH,
        )
        copy.start()
        gathers.append(copy)
    own_load = load(feat_ref.at[local], pieces.at[me_feat], 0)

    tile_load.wait()
    slot_count = counts_ref[local]
    strip = 2 * SUBLANES
    places = []
    for slot in range(slot_total):
        place = rows_ref[local, slot] * block_count + cols_ref[local, slot]
        place = jnp.where(slot < slot_count, place, -1)
        places.append(jnp.full((strip, tile_side), place, jnp.int32))

    def build(at, carry):
        first = pl.multiple_of(at * strip, strip)
        listed = [
            tiles[slot, pl.ds(first, strip), :].astype(jnp.float32) for slot in range(slot_total)
        ]
        for row in range(block_count):
            for col in range(block_count):
                summed = jnp.zeros((strip, tile_side), jnp.float32)
                for slot in range(slot_total):
                    summed += jnp.where(
                        places[slot] == row * block_count + col, listed[slot], 0.0
                    )
                start = pl.multiple_of(row * tile_side + first, strip)
                adjacency[pl.ds(start, strip), col * tile_side : (col + 1) * tile_side] = (
                    summed.astype(jnp.bfloat16)
                )
        return carry

    lax.fori_loop(0, tile_side // strip, build, 0)

    for copy in weight_loads:
        copy.wait()
    for copy in gathers:
        copy.wait_recv()
    own_load.wait()
    features[...] = jnp.transpose(pieces[...].reshape(width, vert_count))

    def mix(lhs, source, before, weight):
        spread = jnp.dot(lhs, source, preferred_element_type=jnp.float32)
        mixed = jnp.dot(
            spread.astype(jnp.bfloat16), weight, preferred_element_type=jnp.float32
        )
        return (before.astype(jnp.float32) + jnp.maximum(mixed, 0.0)).astype(jnp.bfloat16)

    hidden_one[...] = mix(adjacency[...], features[...], features[...], weights[0])
    own_rows = pl.ds(pl.multiple_of(part * part_rows, part_rows), part_rows)
    hidden_two[...] = mix(
        adjacency[own_rows, :], hidden_one[...], hidden_one[own_rows, :], weights[1]
    ).reshape(snaps, vert_dev, width)

    sends = []
    for step in range(1, snaps):
        peer = (own + step) % snaps
        copy = pltpu.make_async_remote_copy(
            src_ref=hidden_two.at[peer],
            dst_ref=vertex_rows.at[own],
            send_sem=spread_send.at[step],
            recv_sem=spread_recv.at[step],
            device_id=(peer // snap_dev, (peer % snap_dev) * parts + part),
            device_id_type=MESH,
        )
        copy.start()
        sends.append(copy)
    vertex_rows[own] = hidden_two[own]
    for copy in sends:
        copy.wait_recv()

    flat = vertex_rows[...].reshape(snaps * vert_dev, width)
    group_rows = snaps * SUBLANES
    groups = vert_dev // SUBLANES

    def split(array):
        array = array.reshape(snaps, groups, SUBLANES, width)
        return [array[:, at].reshape(group_rows, width) for at in range(groups)]

    def project(at):
        return split(jnp.dot(flat, weights[at], preferred_element_type=jnp.float32))

    queries, keys, values = project(2), project(3), project(4)
    before = split(flat.astype(jnp.float32))
    lane_head = lax.broadcasted_iota(jnp.int32, (group_rows, width), 1) // head_dim
    row_at = lax.broadcasted_iota(jnp.int32, (group_rows, group_rows), 0)
    col_at = lax.broadcasted_iota(jnp.int32, (group_rows, group_rows), 1)
    visible = (row_at % SUBLANES == col_at % SUBLANES) & (
        col_at // SUBLANES <= row_at // SUBLANES
    )
    factor = head_dim ** (-0.5) * math.log2(math.e)
    results = []
    for at in range(groups):
        key = keys[at].astype(jnp.bfloat16)
        value = values[at].astype(jnp.bfloat16)
        query = jnp.concatenate(
            [
                jnp.where(lane_head == head, queries[at], 0.0).astype(jnp.bfloat16)
                for head in range(HEADS)
            ],
            axis=0,
        )
        scores = lax.dot_general(
            query, key, (((1,), (1,)), ((), ())), preferred_element_type=jnp.float32
        )
        attention = []
        for head in range(HEADS):
            score = scores[head * group_rows : (head + 1) * group_rows]
            score = jnp.where(visible, score, masked_score)
            lifted = jnp.exp2((score - jnp.max(score, axis=-1, keepdims=True)) * factor)
            scale = 1.0 / jnp.sum(lifted, axis=-1, keepdims=True)
            attention.append((lifted * scale).astype(jnp.bfloat16))
        context_all = jnp.dot(
            jnp.concatenate(attention, axis=0), value, preferred_element_type=jnp.float32
        )
        context = context_all[:group_rows]
        for head in range(1, HEADS):
            context = jnp.where(
                lane_head == head, context_all[head * group_rows : (head + 1) * group_rows], context
            )
        result = before[at] + jnp.dot(
            context.astype(jnp.bfloat16), weights[5], preferred_element_type=jnp.float32
        )
        results.append(result.reshape(snaps, 1, SUBLANES, width))
    evolved = jnp.concatenate(results, axis=1).reshape(n_snap, snap_dev, vert_dev, width)

    low = lax.broadcasted_iota(jnp.int32, (n_snap * vert_dev, LANES), 1) < feat_width
    for at in range(0, n_feat, 2):
        lanes = slice(at * feat_width, (at + 2) * feat_width)
        first = evolved[:, 0, :, lanes].reshape(n_snap * vert_dev, LANES)
        second = evolved[:, 1, :, lanes].reshape(n_snap * vert_dev, LANES)
        even = jnp.where(low, first, pltpu.roll(second, feat_width, 1))
        odd = jnp.where(low, pltpu.roll(first, feat_width, 1), second)
        outgoing[at] = even.astype(jnp.bfloat16).reshape(n_snap, vert_dev, LANES)
        outgoing[at + 1] = odd.astype(jnp.bfloat16).reshape(n_snap, vert_dev, LANES)

    returns = []
    for step in range(1, total):
        peer = (me + step) % total
        copy = pltpu.make_async_remote_copy(
            src_ref=outgoing.at[peer % n_feat, peer // n_feat],
            dst_ref=returned.at[part, own],
            send_sem=return_send.at[step],
            recv_sem=return_recv.at[step],
            device_id=(peer // n_feat, peer % n_feat),
            device_id_type=MESH,
        )
        copy.start()
        returns.append(copy)
    returned[part, own] = outgoing[me_feat, me_snap]
    for copy in gathers + sends:
        copy.wait_send()
    for copy in returns:
        copy.wait_recv()
    out_ref[...] = jnp.transpose(returned[...].reshape(vert_count, LANES)).reshape(
        snap_dev, feat_width, vert_count
    )
    for copy in returns:
        copy.wait_send()


def on_device_fused(n_snap, n_feat, *operands):
    node_features, _, _, _, tile_values, layer_one = operands[:6]
    snap_dev, vert_count, feat_width = node_features.shape
    _, slot_total, tile_side, _ = tile_values.shape
    width = layer_one.shape[0]
    parts = n_feat // snap_dev
    snaps = n_snap * snap_dev
    vert_dev = vert_count // (parts * snaps)
    total = n_snap * n_feat
    kept = jnp.bfloat16
    result = pl.pallas_call(
        functools.partial(fused_kernel, n_snap, n_feat),
        out_shape=jax.ShapeDtypeStruct((snap_dev, feat_width, vert_count), kept),
        in_specs=[pl.BlockSpec(memory_space=pltpu.SMEM)] * 3
        + [pl.BlockSpec(memory_space=pl.ANY)] * 8,
        out_specs=pl.BlockSpec(memory_space=pltpu.VMEM),
        scratch_shapes=[
            pltpu.VMEM((slot_total, tile_side, tile_side), kept),
            pltpu.VMEM((6, width, width), kept),
            pltpu.VMEM((n_feat, feat_width, vert_count), kept),
            pltpu.VMEM((vert_count, vert_count), kept),
            pltpu.VMEM((vert_count, width), kept),
            pltpu.VMEM((vert_count, width), kept),
            pltpu.VMEM((snaps, vert_dev, width), kept),
            pltpu.VMEM((snaps, vert_dev, width), kept),
            pltpu.VMEM((n_feat, n_snap, vert_dev, LANES), kept),
            pltpu.VMEM((parts, snaps, vert_dev, LANES), kept),
            pltpu.SemaphoreType.DMA((8,)),
            pltpu.SemaphoreType.DMA((n_feat,)),
            pltpu.SemaphoreType.DMA((n_feat,)),
            pltpu.SemaphoreType.DMA((snaps,)),
            pltpu.SemaphoreType.DMA((snaps,)),
            pltpu.SemaphoreType.DMA((total,)),
            pltpu.SemaphoreType.DMA((total,)),
        ],
        compiler_params=pltpu.CompilerParams(collective_id=0, has_side_effects=True),
    )(*operands[1:4], node_features.transpose(0, 2, 1), *operands[4:])
    return result.transpose(0, 2, 1)


def dispatch(n_snap, n_feat, *operands):
    snap_dev, vert_count, feat_width = operands[0].shape
    slot_total = operands[4].shape[1]
    snaps = n_snap * snap_dev
    fits = (
        snap_dev == 2
        and 2 * feat_width == LANES
        and n_feat % snap_dev == 0
        and n_feat % 2 == 0
        and vert_count % (n_feat // snap_dev * snaps * 2 * SUBLANES) == 0
        and snaps * SUBLANES == LANES
        and slot_total <= 16
        and vert_count <= 1024
    )
    if fits:
        return on_device_fused(n_snap, n_feat, *operands)
    return on_device(*operands)


def solution(mesh):
    placed = (
        P("snap", None, "feat"),
        P("snap", None),
        P("snap", None),
        P("snap"),
        P("snap", None, None, None),
        P(),
        P(),
        P(),
        P(),
        P(),
        P(),
    )
    return jax.shard_map(
        functools.partial(dispatch, mesh.shape["snap"], mesh.shape["feat"]), mesh=mesh, in_specs=placed, out_specs=P("snap", None, "feat"), check_vma=False
    )
```

```python
import functools
import math

import jax
import jax.numpy as jnp
from jax import lax
from jax.experimental import pallas as pl
from jax.experimental.pallas import tpu as pltpu
from jax.sharding import PartitionSpec as P

HEADS = 8


masked_score = -1e30


def spread_padded(features, tile_block, block_rows, block_cols, slot_count):
    vert_count, feat_width = features.shape
    tile_side = tile_block.shape[1]
    slot_total = tile_block.shape[0]
    block_count = vert_count // tile_side
    blocked = features.reshape(block_count, tile_side, feat_width)
    picked_blocks = blocked[block_cols]
    live_slots = jnp.arange(slot_total, dtype=jnp.int32) < slot_count
    products = jnp.einsum(
        "irc,icf->irf", tile_block, picked_blocks, preferred_element_type=jnp.float32
    )
    products = products * live_slots.astype(jnp.float32)[:, None, None]
    membership = (
        (block_rows[None, :] == jnp.arange(block_count, dtype=jnp.int32)[:, None])
        & live_slots[None, :]
    ).astype(jnp.float32)
    summed = jnp.dot(
        membership,
        products.reshape(slot_total, tile_side * feat_width),
        precision=lax.Precision.HIGHEST,
    )
    return summed.reshape(vert_count, feat_width).astype(jnp.bfloat16)


def attend_local(hidden, query_weight, key_weight, value_weight, out_weight):
    snaps, verts, model_width = hidden.shape
    head_dim = model_width // HEADS
    flat = hidden.reshape(snaps * verts, model_width)

    def project(weight):
        return (
            jnp.dot(flat, weight, preferred_element_type=jnp.float32)
            .astype(jnp.bfloat16)
            .reshape(snaps, verts, HEADS, head_dim)
        )

    query_heads = project(query_weight)
    key_heads = project(key_weight)
    value_heads = project(value_weight)
    scores = jnp.einsum(
        "tvhd,uvhd->vhtu", query_heads, key_heads, preferred_element_type=jnp.float32
    ) * head_dim ** (-0.5)
    causal = (
        jnp.arange(snaps, dtype=jnp.int32)[:, None] >= jnp.arange(snaps, dtype=jnp.int32)[None, :]
    )
    scores = jnp.where(causal, scores, masked_score)
    row_max = jnp.max(scores, axis=-1, keepdims=True)
    lifted = jnp.exp(scores - row_max)
    weights = (lifted / jnp.sum(lifted, axis=-1, keepdims=True)).astype(jnp.bfloat16)
    context = jnp.einsum(
        "vhtu,uvhd->tvhd", weights, value_heads, preferred_element_type=jnp.float32
    ).astype(jnp.bfloat16)
    context = context.reshape(snaps * verts, model_width)
    result = flat.astype(jnp.float32) + jnp.dot(
        context, out_weight, preferred_element_type=jnp.float32
    )
    return result.astype(jnp.bfloat16).reshape(snaps, verts, model_width)


def on_device(
    node_features,
    tile_rows,
    tile_cols,
    tile_counts,
    tile_values,
    layer_one,
    layer_two,
    query_weight,
    key_weight,
    value_weight,
    out_weight,
):
    snap_dev, vert_count, feat_width = node_features.shape
    feat_index = lax.axis_index("feat")

    def spread_all(features):
        spread_pieces = []
        for snapshot in range(snap_dev):
            spread_pieces.append(
                spread_padded(
                    features[snapshot],
                    tile_values[snapshot],
                    tile_rows[snapshot],
                    tile_cols[snapshot],
                    tile_counts[snapshot],
                )
            )
        return jnp.stack(spread_pieces, axis=0)

    def convolve(features, weight):
        spread_rows = spread_all(features).reshape(snap_dev * vert_count, feat_width)
        own_columns = lax.dynamic_slice_in_dim(weight, feat_index * feat_width, feat_width, 1)
        mixed_sum = jnp.dot(
            lax.all_gather(spread_rows, "feat", axis=1, tiled=True),
            own_columns,
            preferred_element_type=jnp.float32,
        )
        mixed_sum = mixed_sum.reshape(snap_dev, vert_count, feat_width)
        return (features.astype(jnp.float32) + jnp.maximum(mixed_sum, 0.0)).astype(jnp.bfloat16)

    hidden_one = convolve(node_features, layer_one)
    hidden_two = convolve(hidden_one, layer_two)
    vertex_rows = lax.all_to_all(
        lax.all_to_all(hidden_two, "snap", split_axis=1, concat_axis=0, tiled=True),
        "feat",
        split_axis=1,
        concat_axis=2,
        tiled=True,
    )
    attended = attend_local(vertex_rows, query_weight, key_weight, value_weight, out_weight)
    return lax.all_to_all(
        lax.all_to_all(attended, "feat", split_axis=2, concat_axis=1, tiled=True),
        "snap",
        split_axis=0,
        concat_axis=1,
        tiled=True,
    )


LANES = 128
SUBLANES = 8
MESH = pl.DeviceIdType.MESH


def fused_kernel(
    n_snap,
    n_feat,
    rows_ref,
    cols_ref,
    counts_ref,
    feat_ref,
    tiles_ref,
    w_one,
    w_two,
    w_query,
    w_key,
    w_value,
    w_out,
    out_ref,
    tiles,
    weights,
    pieces,
    adjacency,
    features,
    hidden_one,
    hidden_two,
    vertex_rows,
    outgoing,
    returned,
    load_sem,
    gather_send,
    gather_recv,
    spread_send,
    spread_recv,
    return_send,
    return_recv,
    heard,
):
    snap_dev, feat_width, vert_count = feat_ref.shape
    slot_total, tile_side, _ = tiles.shape
    block_count = vert_count // tile_side
    snaps, vert_dev, width = vertex_rows.shape
    parts = n_feat // snap_dev
    part_rows = vert_count // parts
    total = n_snap * n_feat
    head_dim = width // HEADS

    me_snap = lax.axis_index("snap")
    me_feat = lax.axis_index("feat")
    me = me_snap * n_feat + me_feat
    part = me_feat % parts
    local = me_feat // parts
    own = me_snap * snap_dev + local

    def load(source, target, at):
        copy = pltpu.make_async_copy(source, target, load_sem.at[at])
        copy.start()
        return copy

    tile_load = load(tiles_ref.at[local], tiles, 1)
    weight_loads = [
        load(ref, weights.at[at], 2 + at)
        for at, ref in enumerate((w_one, w_two, w_query, w_key, w_value, w_out))
    ]

    barrier = pltpu.get_barrier_semaphore()
    twin = me_snap + 1 - 2 * (me_snap % 2)
    ring = [(me_snap + 2) % n_snap, (me_snap + n_snap - 2) % n_snap]
    mates = [(me_feat + step) % n_feat for step in range(1, n_feat)]

    def tell(semaphore, peers):
        for peer in peers:
            pl.semaphore_signal(semaphore, inc=1, device_id=peer, device_id_type=MESH)

    ring_peers = [(peer, me_feat) for peer in ring]
    twin_peer = [(twin, me_feat)]
    mate_peers = [(me_snap, mate) for mate in mates]
    tell(barrier, ring_peers + twin_peer + mate_peers)
    pl.semaphore_wait(barrier, len(ring_peers) + 1 + len(mate_peers))

    gathers = []
    for step in [n_feat // 2] + [s for s in range(1, n_feat) if s != n_feat // 2]:
        peer = (me_feat + step) % n_feat
        copy = pltpu.make_async_remote_copy(
            src_ref=feat_ref.at[peer // parts],
            dst_ref=pieces.at[me_feat],
            send_sem=gather_send.at[step],
            recv_sem=gather_recv.at[step],
            device_id=(me_snap, peer),
            device_id_type=MESH,
        )
        copy.start()
        gathers.append(copy)
    own_load = load(feat_ref.at[local], pieces.at[me_feat], 0)

    hops = n_snap // 4 - 1
    for hop in range(hops):
        tell(heard.at[hop], ring_peers)
        if hop + 1 < hops:
            pl.semaphore_wait(heard.at[hop], len(ring_peers))

    tile_load.wait()
    slot_count = counts_ref[local]
    strip = 2 * SUBLANES
    places = []
    for slot in range(slot_total):
        place = rows_ref[local, slot] * block_count + cols_ref[local, slot]
        place = jnp.where(slot < slot_count, place, -1)
        places.append(jnp.full((strip, tile_side), place, jnp.int32))

    def build(at, carry):
        first = pl.multiple_of(at * strip, strip)
        listed = [
            tiles[slot, pl.ds(first, strip), :].astype(jnp.float32) for slot in range(slot_total)
        ]
        for row in range(block_count):
            for col in range(block_count):
                summed = jnp.zeros((strip, tile_side), jnp.float32)
                for slot in range(slot_total):
                    summed += jnp.where(
                        places[slot] == row * block_count + col, listed[slot], 0.0
                    )
                start = pl.multiple_of(row * tile_side + first, strip)
                adjacency[pl.ds(start, strip), col * tile_side : (col + 1) * tile_side] = (
                    summed.astype(jnp.bfloat16)
                )
        return carry

    strips = tile_side // strip
    lax.fori_loop(0, strips // 2, build, 0)
    pl.semaphore_wait(heard.at[hops - 1], len(ring_peers))
    tell(heard.at[hops], twin_peer)
    lax.fori_loop(strips // 2, strips, build, 0)
    pl.semaphore_wait(heard.at[hops], 1)
    tell(heard.at[hops + 1], mate_peers)

    for copy in weight_loads:
        copy.wait()
    for copy in gathers:
        copy.wait_recv()
    own_load.wait()
    features[...] = jnp.transpose(pieces[...].reshape(width, vert_count))

    def mix(lhs, source, before, weight):
        spread = jnp.dot(lhs, source, preferred_element_type=jnp.float32)
        mixed = jnp.dot(
            spread.astype(jnp.bfloat16), weight, preferred_element_type=jnp.float32
        )
        return (before.astype(jnp.float32) + jnp.maximum(mixed, 0.0)).astype(jnp.bfloat16)

    hidden_one[...] = mix(adjacency[...], features[...], features[...], weights[0])
    own_rows = pl.ds(pl.multiple_of(part * part_rows, part_rows), part_rows)
    hidden_two[...] = mix(
        adjacency[own_rows, :], hidden_one[...], hidden_one[own_rows, :], weights[1]
    ).reshape(snaps, vert_dev, width)

    pl.semaphore_wait(heard.at[hops + 1], len(mate_peers))

    sends = []
    for step in sorted(range(1, snaps), key=lambda s: abs(2 * s - snaps)):
        peer = (own + step) % snaps
        copy = pltpu.make_async_remote_copy(
            src_ref=hidden_two.at[peer],
            dst_ref=vertex_rows.at[own],
            send_sem=spread_send.at[step],
            recv_sem=spread_recv.at[step],
            device_id=(peer // snap_dev, (peer % snap_dev) * parts + part),
            device_id_type=MESH,
        )
        copy.start()
        sends.append(copy)
    vertex_rows[own] = hidden_two[own]
    for copy in sends:
        copy.wait_recv()

    flat = vertex_rows[...].reshape(snaps * vert_dev, width)
    group_rows = snaps * SUBLANES
    groups = vert_dev // SUBLANES

    def split(array):
        array = array.reshape(snaps, groups, SUBLANES, width)
        return [array[:, at].reshape(group_rows, width) for at in range(groups)]

    def project(at):
        return split(jnp.dot(flat, weights[at], preferred_element_type=jnp.float32))

    queries, keys, values = project(2), project(3), project(4)
    before = split(flat.astype(jnp.float32))
    lane_head = lax.broadcasted_iota(jnp.int32, (group_rows, width), 1) // head_dim
    row_at = lax.broadcasted_iota(jnp.int32, (group_rows, group_rows), 0)
    col_at = lax.broadcasted_iota(jnp.int32, (group_rows, group_rows), 1)
    visible = (row_at % SUBLANES == col_at % SUBLANES) & (
        col_at // SUBLANES <= row_at // SUBLANES
    )
    factor = head_dim ** (-0.5) * math.log2(math.e)
    results = []
    for at in range(groups):
        key = keys[at].astype(jnp.bfloat16)
        value = values[at].astype(jnp.bfloat16)
        query = jnp.concatenate(
            [
                jnp.where(lane_head == head, queries[at], 0.0).astype(jnp.bfloat16)
                for head in range(HEADS)
            ],
            axis=0,
        )
        scores = lax.dot_general(
            query, key, (((1,), (1,)), ((), ())), preferred_element_type=jnp.float32
        )
        attention = []
        for head in range(HEADS):
            score = scores[head * group_rows : (head + 1) * group_rows]
            score = jnp.where(visible, score, masked_score)
            lifted = jnp.exp2((score - jnp.max(score, axis=-1, keepdims=True)) * factor)
            scale = 1.0 / jnp.sum(lifted, axis=-1, keepdims=True)
            attention.append((lifted * scale).astype(jnp.bfloat16))
        context_all = jnp.dot(
            jnp.concatenate(attention, axis=0), value, preferred_element_type=jnp.float32
        )
        context = context_all[:group_rows]
        for head in range(1, HEADS):
            context = jnp.where(
                lane_head == head, context_all[head * group_rows : (head + 1) * group_rows], context
            )
        result = before[at] + jnp.dot(
            context.astype(jnp.bfloat16), weights[5], preferred_element_type=jnp.float32
        )
        results.append(result.reshape(snaps, 1, SUBLANES, width))
    evolved = jnp.concatenate(results, axis=1).reshape(n_snap, snap_dev, vert_dev, width)

    low = lax.broadcasted_iota(jnp.int32, (n_snap * vert_dev, LANES), 1) < feat_width
    for at in range(0, n_feat, 2):
        lanes = slice(at * feat_width, (at + 2) * feat_width)
        first = evolved[:, 0, :, lanes].reshape(n_snap * vert_dev, LANES)
        second = evolved[:, 1, :, lanes].reshape(n_snap * vert_dev, LANES)
        even = jnp.where(low, first, pltpu.roll(second, feat_width, 1))
        odd = jnp.where(low, pltpu.roll(first, feat_width, 1), second)
        outgoing[at] = even.astype(jnp.bfloat16).reshape(n_snap, vert_dev, LANES)
        outgoing[at + 1] = odd.astype(jnp.bfloat16).reshape(n_snap, vert_dev, LANES)

    returns = []
    for step in sorted(range(1, total), key=lambda s: abs(2 * s - total)):
        peer = (me + step) % total
        copy = pltpu.make_async_remote_copy(
            src_ref=outgoing.at[peer % n_feat, peer // n_feat],
            dst_ref=returned.at[part, own],
            send_sem=return_send.at[step],
            recv_sem=return_recv.at[step],
            device_id=(peer // n_feat, peer % n_feat),
            device_id_type=MESH,
        )
        copy.start()
        returns.append(copy)
    returned[part, own] = outgoing[me_feat, me_snap]
    for copy in gathers + sends:
        copy.wait_send()
    for copy in returns:
        copy.wait_recv()
    out_ref[...] = jnp.transpose(returned[...].reshape(vert_count, LANES)).reshape(
        snap_dev, feat_width, vert_count
    )
    for copy in returns:
        copy.wait_send()


def on_device_fused(n_snap, n_feat, *operands):
    node_features, _, _, _, tile_values, layer_one = operands[:6]
    snap_dev, vert_count, feat_width = node_features.shape
    _, slot_total, tile_side, _ = tile_values.shape
    width = layer_one.shape[0]
    parts = n_feat // snap_dev
    snaps = n_snap * snap_dev
    vert_dev = vert_count // (parts * snaps)
    total = n_snap * n_feat
    kept = jnp.bfloat16
    result = pl.pallas_call(
        functools.partial(fused_kernel, n_snap, n_feat),
        out_shape=jax.ShapeDtypeStruct((snap_dev, feat_width, vert_count), kept),
        in_specs=[pl.BlockSpec(memory_space=pltpu.SMEM)] * 3
        + [pl.BlockSpec(memory_space=pl.ANY)] * 8,
        out_specs=pl.BlockSpec(memory_space=pltpu.VMEM),
        scratch_shapes=[
            pltpu.VMEM((slot_total, tile_side, tile_side), kept),
            pltpu.VMEM((6, width, width), kept),
            pltpu.VMEM((n_feat, feat_width, vert_count), kept),
            pltpu.VMEM((vert_count, vert_count), kept),
            pltpu.VMEM((vert_count, width), kept),
            pltpu.VMEM((vert_count, width), kept),
            pltpu.VMEM((snaps, vert_dev, width), kept),
            pltpu.VMEM((snaps, vert_dev, width), kept),
            pltpu.VMEM((n_feat, n_snap, vert_dev, LANES), kept),
            pltpu.VMEM((parts, snaps, vert_dev, LANES), kept),
            pltpu.SemaphoreType.DMA((8,)),
            pltpu.SemaphoreType.DMA((n_feat,)),
            pltpu.SemaphoreType.DMA((n_feat,)),
            pltpu.SemaphoreType.DMA((snaps,)),
            pltpu.SemaphoreType.DMA((snaps,)),
            pltpu.SemaphoreType.DMA((total,)),
            pltpu.SemaphoreType.DMA((total,)),
            pltpu.SemaphoreType.REGULAR((n_snap // 4 + 1,)),
        ],
        compiler_params=pltpu.CompilerParams(collective_id=0, has_side_effects=True),
    )(*operands[1:4], node_features.transpose(0, 2, 1), *operands[4:])
    return result.transpose(0, 2, 1)


def dispatch(n_snap, n_feat, *operands):
    snap_dev, vert_count, feat_width = operands[0].shape
    slot_total = operands[4].shape[1]
    snaps = n_snap * snap_dev
    fits = (
        snap_dev == 2
        and 2 * feat_width == LANES
        and n_feat % snap_dev == 0
        and n_feat % 2 == 0
        and n_snap >= 8
        and n_snap % 4 == 0
        and vert_count % (n_feat // snap_dev * snaps * 2 * SUBLANES) == 0
        and snaps * SUBLANES == LANES
        and slot_total <= 16
        and vert_count <= 1024
    )
    if fits:
        return on_device_fused(n_snap, n_feat, *operands)
    return on_device(*operands)


def solution(mesh):
    placed = (
        P("snap", None, "feat"),
        P("snap", None),
        P("snap", None),
        P("snap"),
        P("snap", None, None, None),
        P(),
        P(),
        P(),
        P(),
        P(),
        P(),
    )
    return jax.shard_map(
        functools.partial(dispatch, mesh.shape["snap"], mesh.shape["feat"]), mesh=mesh, in_specs=placed, out_specs=P("snap", None, "feat"), check_vma=False
    )
```

```python
import functools
import math

import jax
import jax.numpy as jnp
from jax import lax
from jax.experimental import pallas as pl
from jax.experimental.pallas import tpu as pltpu
from jax.sharding import PartitionSpec as P

HEADS = 8


masked_score = -1e30


def spread_padded(features, tile_block, block_rows, block_cols, slot_count):
    vert_count, feat_width = features.shape
    tile_side = tile_block.shape[1]
    slot_total = tile_block.shape[0]
    block_count = vert_count // tile_side
    blocked = features.reshape(block_count, tile_side, feat_width)
    picked_blocks = blocked[block_cols]
    live_slots = jnp.arange(slot_total, dtype=jnp.int32) < slot_count
    products = jnp.einsum(
        "irc,icf->irf", tile_block, picked_blocks, preferred_element_type=jnp.float32
    )
    products = products * live_slots.astype(jnp.float32)[:, None, None]
    membership = (
        (block_rows[None, :] == jnp.arange(block_count, dtype=jnp.int32)[:, None])
        & live_slots[None, :]
    ).astype(jnp.float32)
    summed = jnp.dot(
        membership,
        products.reshape(slot_total, tile_side * feat_width),
        precision=lax.Precision.HIGHEST,
    )
    return summed.reshape(vert_count, feat_width).astype(jnp.bfloat16)


def attend_local(hidden, query_weight, key_weight, value_weight, out_weight):
    snaps, verts, model_width = hidden.shape
    head_dim = model_width // HEADS
    flat = hidden.reshape(snaps * verts, model_width)

    def project(weight):
        return (
            jnp.dot(flat, weight, preferred_element_type=jnp.float32)
            .astype(jnp.bfloat16)
            .reshape(snaps, verts, HEADS, head_dim)
        )

    query_heads = project(query_weight)
    key_heads = project(key_weight)
    value_heads = project(value_weight)
    scores = jnp.einsum(
        "tvhd,uvhd->vhtu", query_heads, key_heads, preferred_element_type=jnp.float32
    ) * head_dim ** (-0.5)
    causal = (
        jnp.arange(snaps, dtype=jnp.int32)[:, None] >= jnp.arange(snaps, dtype=jnp.int32)[None, :]
    )
    scores = jnp.where(causal, scores, masked_score)
    row_max = jnp.max(scores, axis=-1, keepdims=True)
    lifted = jnp.exp(scores - row_max)
    weights = (lifted / jnp.sum(lifted, axis=-1, keepdims=True)).astype(jnp.bfloat16)
    context = jnp.einsum(
        "vhtu,uvhd->tvhd", weights, value_heads, preferred_element_type=jnp.float32
    ).astype(jnp.bfloat16)
    context = context.reshape(snaps * verts, model_width)
    result = flat.astype(jnp.float32) + jnp.dot(
        context, out_weight, preferred_element_type=jnp.float32
    )
    return result.astype(jnp.bfloat16).reshape(snaps, verts, model_width)


def on_device(
    node_features,
    tile_rows,
    tile_cols,
    tile_counts,
    tile_values,
    layer_one,
    layer_two,
    query_weight,
    key_weight,
    value_weight,
    out_weight,
):
    snap_dev, vert_count, feat_width = node_features.shape
    feat_index = lax.axis_index("feat")

    def spread_all(features):
        spread_pieces = []
        for snapshot in range(snap_dev):
            spread_pieces.append(
                spread_padded(
                    features[snapshot],
                    tile_values[snapshot],
                    tile_rows[snapshot],
                    tile_cols[snapshot],
                    tile_counts[snapshot],
                )
            )
        return jnp.stack(spread_pieces, axis=0)

    def convolve(features, weight):
        spread_rows = spread_all(features).reshape(snap_dev * vert_count, feat_width)
        own_columns = lax.dynamic_slice_in_dim(weight, feat_index * feat_width, feat_width, 1)
        mixed_sum = jnp.dot(
            lax.all_gather(spread_rows, "feat", axis=1, tiled=True),
            own_columns,
            preferred_element_type=jnp.float32,
        )
        mixed_sum = mixed_sum.reshape(snap_dev, vert_count, feat_width)
        return (features.astype(jnp.float32) + jnp.maximum(mixed_sum, 0.0)).astype(jnp.bfloat16)

    hidden_one = convolve(node_features, layer_one)
    hidden_two = convolve(hidden_one, layer_two)
    vertex_rows = lax.all_to_all(
        lax.all_to_all(hidden_two, "snap", split_axis=1, concat_axis=0, tiled=True),
        "feat",
        split_axis=1,
        concat_axis=2,
        tiled=True,
    )
    attended = attend_local(vertex_rows, query_weight, key_weight, value_weight, out_weight)
    return lax.all_to_all(
        lax.all_to_all(attended, "feat", split_axis=2, concat_axis=1, tiled=True),
        "snap",
        split_axis=0,
        concat_axis=1,
        tiled=True,
    )


LANES = 128
SUBLANES = 8
MESH = pl.DeviceIdType.MESH


def fused_kernel(
    n_snap,
    n_feat,
    rows_hbm,
    cols_hbm,
    counts_hbm,
    feat_ref,
    tiles_ref,
    w_one,
    w_two,
    w_query,
    w_key,
    w_value,
    w_out,
    returned,
    tiles,
    weights,
    pieces,
    adjacency,
    features,
    hidden_one,
    hidden_two,
    vertex_rows,
    outgoing,
    load_sem,
    gather_send,
    gather_recv,
    spread_send,
    spread_recv,
    return_send,
    return_recv,
    heard,
    rows_ref,
    cols_ref,
    counts_ref,
):
    snap_dev, feat_width, vert_count = feat_ref.shape
    slot_total, tile_side, _ = tiles.shape
    block_count = vert_count // tile_side
    snaps, vert_dev, width = vertex_rows.shape
    parts = n_feat // snap_dev
    part_rows = vert_count // parts
    total = n_snap * n_feat
    head_dim = width // HEADS

    me_snap = lax.axis_index("snap")
    me_feat = lax.axis_index("feat")
    me = me_snap * n_feat + me_feat
    part = me_feat % parts
    local = me_feat // parts
    own = me_snap * snap_dev + local

    def load(source, target, at):
        copy = pltpu.make_async_copy(source, target, load_sem.at[at])
        copy.start()
        return copy

    list_loads = [
        load(ref, kept, 8 + at)
        for at, (ref, kept) in enumerate(
            ((rows_hbm, rows_ref), (cols_hbm, cols_ref), (counts_hbm, counts_ref))
        )
    ]
    tile_load = load(tiles_ref.at[local], tiles, 1)
    weight_loads = [
        load(ref, weights.at[at], 2 + at)
        for at, ref in enumerate((w_one, w_two, w_query, w_key, w_value, w_out))
    ]

    barrier = pltpu.get_barrier_semaphore()
    twin = me_snap + 1 - 2 * (me_snap % 2)
    ring = [(me_snap + 2) % n_snap, (me_snap + n_snap - 2) % n_snap]
    mates = [(me_feat + step) % n_feat for step in range(1, n_feat)]

    def tell(semaphore, peers):
        for peer in peers:
            pl.semaphore_signal(semaphore, inc=1, device_id=peer, device_id_type=MESH)

    ring_peers = [(peer, me_feat) for peer in ring]
    twin_peer = [(twin, me_feat)]
    mate_peers = [(me_snap, mate) for mate in mates]
    tell(barrier, ring_peers + twin_peer + mate_peers)
    pl.semaphore_wait(barrier, len(ring_peers) + 1 + len(mate_peers))

    gathers = []
    for step in [n_feat // 2] + [s for s in range(1, n_feat) if s != n_feat // 2]:
        peer = (me_feat + step) % n_feat
        copy = pltpu.make_async_remote_copy(
            src_ref=feat_ref.at[peer // parts],
            dst_ref=pieces.at[me_feat],
            send_sem=gather_send.at[step],
            recv_sem=gather_recv.at[step],
            device_id=(me_snap, peer),
            device_id_type=MESH,
        )
        copy.start()
        gathers.append(copy)
    own_load = load(feat_ref.at[local], pieces.at[me_feat], 0)

    hops = n_snap // 4 - 1
    for hop in range(hops):
        tell(heard.at[hop], ring_peers)
        if hop + 1 < hops:
            pl.semaphore_wait(heard.at[hop], len(ring_peers))

    tile_load.wait()
    for copy in list_loads:
        copy.wait()
    slot_count = counts_ref[local]
    strip = 2 * SUBLANES
    places = []
    for slot in range(slot_total):
        place = rows_ref[local, slot] * block_count + cols_ref[local, slot]
        place = jnp.where(slot < slot_count, place, -1)
        places.append(jnp.full((strip, tile_side), place, jnp.int32))

    def build(at, carry):
        first = pl.multiple_of(at * strip, strip)
        listed = [
            tiles[slot, pl.ds(first, strip), :].astype(jnp.float32) for slot in range(slot_total)
        ]
        for row in range(block_count):
            for col in range(block_count):
                summed = jnp.zeros((strip, tile_side), jnp.float32)
                for slot in range(slot_total):
                    summed += jnp.where(
                        places[slot] == row * block_count + col, listed[slot], 0.0
                    )
                start = pl.multiple_of(row * tile_side + first, strip)
                adjacency[pl.ds(start, strip), col * tile_side : (col + 1) * tile_side] = (
                    summed.astype(jnp.bfloat16)
                )
        return carry

    strips = tile_side // strip
    lax.fori_loop(0, strips // 2, build, 0)
    pl.semaphore_wait(heard.at[hops - 1], len(ring_peers))
    tell(heard.at[hops], twin_peer)
    lax.fori_loop(strips // 2, strips, build, 0)
    pl.semaphore_wait(heard.at[hops], 1)
    tell(heard.at[hops + 1], mate_peers)

    for copy in weight_loads:
        copy.wait()
    for copy in gathers:
        copy.wait_recv()
    own_load.wait()
    features[...] = jnp.transpose(pieces[...].reshape(width, vert_count))

    def mix(lhs, source, before, weight):
        spread = jnp.dot(lhs, source, preferred_element_type=jnp.float32)
        mixed = jnp.dot(
            spread.astype(jnp.bfloat16), weight, preferred_element_type=jnp.float32
        )
        return (before.astype(jnp.float32) + jnp.maximum(mixed, 0.0)).astype(jnp.bfloat16)

    hidden_one[...] = mix(adjacency[...], features[...], features[...], weights[0])
    own_rows = pl.ds(pl.multiple_of(part * part_rows, part_rows), part_rows)
    hidden_two[...] = mix(
        adjacency[own_rows, :], hidden_one[...], hidden_one[own_rows, :], weights[1]
    ).reshape(snaps, vert_dev, width)

    pl.semaphore_wait(heard.at[hops + 1], len(mate_peers))

    sends = []
    for step in sorted(range(1, snaps), key=lambda s: abs(2 * s - snaps)):
        peer = (own + step) % snaps
        copy = pltpu.make_async_remote_copy(
            src_ref=hidden_two.at[peer],
            dst_ref=vertex_rows.at[own],
            send_sem=spread_send.at[step],
            recv_sem=spread_recv.at[step],
            device_id=(peer // snap_dev, (peer % snap_dev) * parts + part),
            device_id_type=MESH,
        )
        copy.start()
        sends.append(copy)
    vertex_rows[own] = hidden_two[own]
    for copy in sends:
        copy.wait_recv()

    flat = vertex_rows[...].reshape(snaps * vert_dev, width)
    group_rows = snaps * SUBLANES
    groups = vert_dev // SUBLANES

    def split(array):
        array = array.reshape(snaps, groups, SUBLANES, width)
        return [array[:, at].reshape(group_rows, width) for at in range(groups)]

    def project(at):
        return split(jnp.dot(flat, weights[at], preferred_element_type=jnp.float32))

    queries, keys, values = project(2), project(3), project(4)
    before = split(flat.astype(jnp.float32))
    lane_head = lax.broadcasted_iota(jnp.int32, (group_rows, width), 1) // head_dim
    row_at = lax.broadcasted_iota(jnp.int32, (group_rows, group_rows), 0)
    col_at = lax.broadcasted_iota(jnp.int32, (group_rows, group_rows), 1)
    visible = (row_at % SUBLANES == col_at % SUBLANES) & (
        col_at // SUBLANES <= row_at // SUBLANES
    )
    factor = head_dim ** (-0.5) * math.log2(math.e)
    results = []
    for at in range(groups):
        key = keys[at].astype(jnp.bfloat16)
        value = values[at].astype(jnp.bfloat16)
        query = jnp.concatenate(
            [
                jnp.where(lane_head == head, queries[at], 0.0).astype(jnp.bfloat16)
                for head in range(HEADS)
            ],
            axis=0,
        )
        scores = lax.dot_general(
            query, key, (((1,), (1,)), ((), ())), preferred_element_type=jnp.float32
        )
        attention = []
        for head in range(HEADS):
            score = scores[head * group_rows : (head + 1) * group_rows]
            score = jnp.where(visible, score, masked_score)
            lifted = jnp.exp2((score - jnp.max(score, axis=-1, keepdims=True)) * factor)
            scale = 1.0 / jnp.sum(lifted, axis=-1, keepdims=True)
            attention.append((lifted * scale).astype(jnp.bfloat16))
        context_all = jnp.dot(
            jnp.concatenate(attention, axis=0), value, preferred_element_type=jnp.float32
        )
        context = context_all[:group_rows]
        for head in range(1, HEADS):
            context = jnp.where(
                lane_head == head, context_all[head * group_rows : (head + 1) * group_rows], context
            )
        result = before[at] + jnp.dot(
            context.astype(jnp.bfloat16), weights[5], preferred_element_type=jnp.float32
        )
        results.append(result.reshape(snaps, 1, SUBLANES, width))
    evolved = jnp.concatenate(results, axis=1).reshape(n_snap, snap_dev, vert_dev, width)

    low = lax.broadcasted_iota(jnp.int32, (n_snap * vert_dev, LANES), 1) < feat_width
    for at in range(0, n_feat, 2):
        lanes = slice(at * feat_width, (at + 2) * feat_width)
        first = evolved[:, 0, :, lanes].reshape(n_snap * vert_dev, LANES)
        second = evolved[:, 1, :, lanes].reshape(n_snap * vert_dev, LANES)
        even = jnp.where(low, first, pltpu.roll(second, feat_width, 1))
        odd = jnp.where(low, pltpu.roll(first, feat_width, 1), second)
        outgoing[at] = even.astype(jnp.bfloat16).reshape(n_snap, vert_dev, LANES)
        outgoing[at + 1] = odd.astype(jnp.bfloat16).reshape(n_snap, vert_dev, LANES)

    returns = []
    for step in sorted(range(1, total), key=lambda s: abs(2 * s - total)):
        peer = (me + step) % total
        copy = pltpu.make_async_remote_copy(
            src_ref=outgoing.at[peer % n_feat, peer // n_feat],
            dst_ref=returned.at[part, own],
            send_sem=return_send.at[step],
            recv_sem=return_recv.at[step],
            device_id=(peer // n_feat, peer % n_feat),
            device_id_type=MESH,
        )
        copy.start()
        returns.append(copy)
    own_copy = load(outgoing.at[me_feat, me_snap], returned.at[part, own], 0)
    for copy in gathers + sends:
        copy.wait_send()
    own_copy.wait()
    for copy in returns:
        copy.wait_recv()
    for copy in returns:
        copy.wait_send()


def on_device_fused(n_snap, n_feat, *operands):
    node_features, _, _, _, tile_values, layer_one = operands[:6]
    snap_dev, vert_count, feat_width = node_features.shape
    _, slot_total, tile_side, _ = tile_values.shape
    width = layer_one.shape[0]
    parts = n_feat // snap_dev
    snaps = n_snap * snap_dev
    vert_dev = vert_count // (parts * snaps)
    total = n_snap * n_feat
    kept = jnp.bfloat16
    result = pl.pallas_call(
        functools.partial(fused_kernel, n_snap, n_feat),
        out_shape=jax.ShapeDtypeStruct((parts, snaps, vert_dev, LANES), kept),
        in_specs=[pl.BlockSpec(memory_space=pltpu.HBM)] * 11,
        out_specs=pl.BlockSpec(memory_space=pl.ANY),
        scratch_shapes=[
            pltpu.VMEM((slot_total, tile_side, tile_side), kept),
            pltpu.VMEM((6, width, width), kept),
            pltpu.VMEM((n_feat, feat_width, vert_count), kept),
            pltpu.VMEM((vert_count, vert_count), kept),
            pltpu.VMEM((vert_count, width), kept),
            pltpu.VMEM((vert_count, width), kept),
            pltpu.VMEM((snaps, vert_dev, width), kept),
            pltpu.VMEM((snaps, vert_dev, width), kept),
            pltpu.VMEM((n_feat, n_snap, vert_dev, LANES), kept),
            pltpu.SemaphoreType.DMA((11,)),
            pltpu.SemaphoreType.DMA((n_feat,)),
            pltpu.SemaphoreType.DMA((n_feat,)),
            pltpu.SemaphoreType.DMA((snaps,)),
            pltpu.SemaphoreType.DMA((snaps,)),
            pltpu.SemaphoreType.DMA((total,)),
            pltpu.SemaphoreType.DMA((total,)),
            pltpu.SemaphoreType.REGULAR((n_snap // 4 + 1,)),
            pltpu.SMEM((snap_dev, slot_total), jnp.int32),
            pltpu.SMEM((snap_dev, slot_total), jnp.int32),
            pltpu.SMEM((snap_dev,), jnp.int32),
        ],
        compiler_params=pltpu.CompilerParams(collective_id=0, has_side_effects=True, vmem_limit_bytes=8388608),
    )(*operands[1:4], node_features.transpose(0, 2, 1), *operands[4:])
    result = jnp.transpose(result.reshape(vert_count, LANES))
    return result.reshape(snap_dev, feat_width, vert_count).transpose(0, 2, 1)


def dispatch(n_snap, n_feat, *operands):
    snap_dev, vert_count, feat_width = operands[0].shape
    slot_total = operands[4].shape[1]
    snaps = n_snap * snap_dev
    fits = (
        snap_dev == 2
        and 2 * feat_width == LANES
        and n_feat % snap_dev == 0
        and n_feat % 2 == 0
        and n_snap >= 8
        and n_snap % 4 == 0
        and vert_count % (n_feat // snap_dev * snaps * 2 * SUBLANES) == 0
        and snaps * SUBLANES == LANES
        and slot_total <= 16
        and vert_count <= 1024
    )
    if fits:
        return on_device_fused(n_snap, n_feat, *operands)
    return on_device(*operands)


def solution(mesh):
    placed = (
        P("snap", None, "feat"),
        P("snap", None),
        P("snap", None),
        P("snap"),
        P("snap", None, None, None),
        P(),
        P(),
        P(),
        P(),
        P(),
        P(),
    )
    return jax.shard_map(
        functools.partial(dispatch, mesh.shape["snap"], mesh.shape["feat"]), mesh=mesh, in_specs=placed, out_specs=P("snap", None, "feat"), check_vma=False
    )
```

```python
import functools
import math

import jax
import jax.numpy as jnp
from jax import lax
from jax.experimental import pallas as pl
from jax.experimental.pallas import tpu as pltpu
from jax.sharding import PartitionSpec as P

HEADS = 8


masked_score = -1e30


def spread_padded(features, tile_block, block_rows, block_cols, slot_count):
    vert_count, feat_width = features.shape
    tile_side = tile_block.shape[1]
    slot_total = tile_block.shape[0]
    block_count = vert_count // tile_side
    blocked = features.reshape(block_count, tile_side, feat_width)
    picked_blocks = blocked[block_cols]
    live_slots = jnp.arange(slot_total, dtype=jnp.int32) < slot_count
    products = jnp.einsum(
        "irc,icf->irf", tile_block, picked_blocks, preferred_element_type=jnp.float32
    )
    products = products * live_slots.astype(jnp.float32)[:, None, None]
    membership = (
        (block_rows[None, :] == jnp.arange(block_count, dtype=jnp.int32)[:, None])
        & live_slots[None, :]
    ).astype(jnp.float32)
    summed = jnp.dot(
        membership,
        products.reshape(slot_total, tile_side * feat_width),
        precision=lax.Precision.HIGHEST,
    )
    return summed.reshape(vert_count, feat_width).astype(jnp.bfloat16)


def attend_local(hidden, query_weight, key_weight, value_weight, out_weight):
    snaps, verts, model_width = hidden.shape
    head_dim = model_width // HEADS
    flat = hidden.reshape(snaps * verts, model_width)

    def project(weight):
        return (
            jnp.dot(flat, weight, preferred_element_type=jnp.float32)
            .astype(jnp.bfloat16)
            .reshape(snaps, verts, HEADS, head_dim)
        )

    query_heads = project(query_weight)
    key_heads = project(key_weight)
    value_heads = project(value_weight)
    scores = jnp.einsum(
        "tvhd,uvhd->vhtu", query_heads, key_heads, preferred_element_type=jnp.float32
    ) * head_dim ** (-0.5)
    causal = (
        jnp.arange(snaps, dtype=jnp.int32)[:, None] >= jnp.arange(snaps, dtype=jnp.int32)[None, :]
    )
    scores = jnp.where(causal, scores, masked_score)
    row_max = jnp.max(scores, axis=-1, keepdims=True)
    lifted = jnp.exp(scores - row_max)
    weights = (lifted / jnp.sum(lifted, axis=-1, keepdims=True)).astype(jnp.bfloat16)
    context = jnp.einsum(
        "vhtu,uvhd->tvhd", weights, value_heads, preferred_element_type=jnp.float32
    ).astype(jnp.bfloat16)
    context = context.reshape(snaps * verts, model_width)
    result = flat.astype(jnp.float32) + jnp.dot(
        context, out_weight, preferred_element_type=jnp.float32
    )
    return result.astype(jnp.bfloat16).reshape(snaps, verts, model_width)


def on_device(
    node_features,
    tile_rows,
    tile_cols,
    tile_counts,
    tile_values,
    layer_one,
    layer_two,
    query_weight,
    key_weight,
    value_weight,
    out_weight,
):
    snap_dev, vert_count, feat_width = node_features.shape
    feat_index = lax.axis_index("feat")

    def spread_all(features):
        spread_pieces = []
        for snapshot in range(snap_dev):
            spread_pieces.append(
                spread_padded(
                    features[snapshot],
                    tile_values[snapshot],
                    tile_rows[snapshot],
                    tile_cols[snapshot],
                    tile_counts[snapshot],
                )
            )
        return jnp.stack(spread_pieces, axis=0)

    def convolve(features, weight):
        spread_rows = spread_all(features).reshape(snap_dev * vert_count, feat_width)
        own_columns = lax.dynamic_slice_in_dim(weight, feat_index * feat_width, feat_width, 1)
        mixed_sum = jnp.dot(
            lax.all_gather(spread_rows, "feat", axis=1, tiled=True),
            own_columns,
            preferred_element_type=jnp.float32,
        )
        mixed_sum = mixed_sum.reshape(snap_dev, vert_count, feat_width)
        return (features.astype(jnp.float32) + jnp.maximum(mixed_sum, 0.0)).astype(jnp.bfloat16)

    hidden_one = convolve(node_features, layer_one)
    hidden_two = convolve(hidden_one, layer_two)
    vertex_rows = lax.all_to_all(
        lax.all_to_all(hidden_two, "snap", split_axis=1, concat_axis=0, tiled=True),
        "feat",
        split_axis=1,
        concat_axis=2,
        tiled=True,
    )
    attended = attend_local(vertex_rows, query_weight, key_weight, value_weight, out_weight)
    return lax.all_to_all(
        lax.all_to_all(attended, "feat", split_axis=2, concat_axis=1, tiled=True),
        "snap",
        split_axis=0,
        concat_axis=1,
        tiled=True,
    )


LANES = 128
SUBLANES = 8
MESH = pl.DeviceIdType.MESH


def fused_kernel(
    n_snap,
    n_feat,
    rows_hbm,
    cols_hbm,
    counts_hbm,
    feat_ref,
    tiles_ref,
    w_one,
    w_two,
    w_query,
    w_key,
    w_value,
    w_out,
    returned,
    tiles,
    weights,
    pieces,
    adjacency,
    features,
    hidden_one,
    hidden_two,
    vertex_rows,
    outgoing,
    load_sem,
    gather_send,
    gather_recv,
    spread_send,
    spread_recv,
    return_send,
    return_recv,
    heard,
    rows_ref,
    cols_ref,
    counts_ref,
):
    snap_dev, feat_width, vert_count = feat_ref.shape
    slot_total, tile_side, _ = tiles.shape
    block_count = vert_count // tile_side
    snaps, vert_dev, width = vertex_rows.shape
    parts = n_feat // snap_dev
    part_rows = vert_count // parts
    total = n_snap * n_feat
    head_dim = width // HEADS

    me_snap = lax.axis_index("snap")
    me_feat = lax.axis_index("feat")
    me = me_snap * n_feat + me_feat
    part = me_feat % parts
    local = me_feat // parts
    own = me_snap * snap_dev + local

    def load(source, target, at):
        copy = pltpu.make_async_copy(source, target, load_sem.at[at])
        copy.start()
        return copy

    list_loads = [
        load(ref, kept, 8 + at)
        for at, (ref, kept) in enumerate(
            ((rows_hbm, rows_ref), (cols_hbm, cols_ref), (counts_hbm, counts_ref))
        )
    ]
    tile_load = load(tiles_ref.at[local], tiles, 1)
    weight_loads = [
        load(ref, weights.at[at], 2 + at)
        for at, ref in enumerate((w_one, w_two, w_query, w_key, w_value, w_out))
    ]

    barrier = pltpu.get_barrier_semaphore()
    twin = me_snap + 1 - 2 * (me_snap % 2)
    ring = [(me_snap + 2) % n_snap, (me_snap + n_snap - 2) % n_snap]
    mates = [(me_feat + step) % n_feat for step in range(1, n_feat)]

    def tell(semaphore, peers):
        for peer in peers:
            pl.semaphore_signal(semaphore, inc=1, device_id=peer, device_id_type=MESH)

    ring_peers = [(peer, me_feat) for peer in ring]
    twin_peer = [(twin, me_feat)]
    mate_peers = [(me_snap, mate) for mate in mates]
    tell(barrier, ring_peers + twin_peer + mate_peers)
    pl.semaphore_wait(barrier, len(ring_peers) + 1 + len(mate_peers))

    gathers = []
    for step in [n_feat // 2] + [s for s in range(1, n_feat) if s != n_feat // 2]:
        peer = (me_feat + step) % n_feat
        copy = pltpu.make_async_remote_copy(
            src_ref=feat_ref.at[peer // parts],
            dst_ref=pieces.at[me_feat],
            send_sem=gather_send.at[step],
            recv_sem=gather_recv.at[step],
            device_id=(me_snap, peer),
            device_id_type=MESH,
        )
        copy.start()
        gathers.append(copy)
    own_load = load(feat_ref.at[local], pieces.at[me_feat], 0)

    hops = n_snap // 4 - 1
    for hop in range(hops):
        tell(heard.at[hop], ring_peers)
        if hop + 1 < hops:
            pl.semaphore_wait(heard.at[hop], len(ring_peers))

    tile_load.wait()
    for copy in list_loads:
        copy.wait()
    slot_count = counts_ref[local]
    strip = 2 * SUBLANES
    places = []
    for slot in range(slot_total):
        place = rows_ref[local, slot] * block_count + cols_ref[local, slot]
        place = jnp.where(slot < slot_count, place, -1)
        places.append(jnp.full((strip, tile_side), place, jnp.int32))

    def build(at, carry):
        first = pl.multiple_of(at * strip, strip)
        listed = [
            tiles[slot, pl.ds(first, strip), :].astype(jnp.float32) for slot in range(slot_total)
        ]
        for row in range(block_count):
            for col in range(block_count):
                summed = jnp.zeros((strip, tile_side), jnp.float32)
                for slot in range(slot_total):
                    summed += jnp.where(
                        places[slot] == row * block_count + col, listed[slot], 0.0
                    )
                start = pl.multiple_of(row * tile_side + first, strip)
                adjacency[pl.ds(start, strip), col * tile_side : (col + 1) * tile_side] = (
                    summed.astype(jnp.bfloat16)
                )
        return carry

    strips = tile_side // strip
    lax.fori_loop(0, strips // 2, build, 0)
    pl.semaphore_wait(heard.at[hops - 1], len(ring_peers))
    tell(heard.at[hops], twin_peer)
    lax.fori_loop(strips // 2, strips, build, 0)
    pl.semaphore_wait(heard.at[hops], 1)
    tell(heard.at[hops + 1], mate_peers)

    for copy in weight_loads:
        copy.wait()
    for copy in gathers:
        copy.wait_recv()
    own_load.wait()
    features[...] = jnp.transpose(pieces[...].reshape(width, vert_count))

    def mix(lhs, source, before, weight):
        spread = jnp.dot(lhs, source, preferred_element_type=jnp.float32)
        mixed = jnp.dot(
            spread.astype(jnp.bfloat16), weight, preferred_element_type=jnp.float32
        )
        return (before.astype(jnp.float32) + jnp.maximum(mixed, 0.0)).astype(jnp.bfloat16)

    hidden_one[...] = mix(adjacency[...], features[...], features[...], weights[0])
    own_rows = pl.ds(pl.multiple_of(part * part_rows, part_rows), part_rows)
    hidden_two[...] = mix(
        adjacency[own_rows, :], hidden_one[...], hidden_one[own_rows, :], weights[1]
    ).reshape(snaps, vert_dev, width)

    pl.semaphore_wait(heard.at[hops + 1], len(mate_peers))

    sends = []
    for step in sorted(range(1, snaps), key=lambda s: abs(2 * s - snaps)):
        peer = (own + step) % snaps
        copy = pltpu.make_async_remote_copy(
            src_ref=hidden_two.at[peer],
            dst_ref=vertex_rows.at[own],
            send_sem=spread_send.at[step],
            recv_sem=spread_recv.at[step],
            device_id=(peer // snap_dev, (peer % snap_dev) * parts + part),
            device_id_type=MESH,
        )
        copy.start()
        sends.append(copy)
    vertex_rows[own] = hidden_two[own]
    for copy in sends:
        copy.wait_recv()

    flat = vertex_rows[...].reshape(snaps * vert_dev, width)
    group_rows = snaps * SUBLANES
    groups = vert_dev // SUBLANES

    def split(array):
        array = array.reshape(snaps, groups, SUBLANES, width)
        return [array[:, at].reshape(group_rows, width) for at in range(groups)]

    def project(at):
        return split(jnp.dot(flat, weights[at], preferred_element_type=jnp.float32))

    queries, keys, values = project(2), project(3), project(4)
    before = split(flat.astype(jnp.float32))
    lane_head = lax.broadcasted_iota(jnp.int32, (group_rows, width), 1) // head_dim
    row_at = lax.broadcasted_iota(jnp.int32, (group_rows, group_rows), 0)
    col_at = lax.broadcasted_iota(jnp.int32, (group_rows, group_rows), 1)
    visible = (row_at % SUBLANES == col_at % SUBLANES) & (
        col_at // SUBLANES <= row_at // SUBLANES
    )
    factor = head_dim ** (-0.5) * math.log2(math.e)
    results = []
    for at in range(groups):
        key = keys[at].astype(jnp.bfloat16)
        value = values[at].astype(jnp.bfloat16)
        query = jnp.concatenate(
            [
                jnp.where(lane_head == head, queries[at], 0.0).astype(jnp.bfloat16)
                for head in range(HEADS)
            ],
            axis=0,
        )
        scores = lax.dot_general(
            query, key, (((1,), (1,)), ((), ())), preferred_element_type=jnp.float32
        )
        attention = []
        for head in range(HEADS):
            score = scores[head * group_rows : (head + 1) * group_rows]
            score = jnp.where(visible, score, masked_score)
            lifted = jnp.exp2((score - jnp.max(score, axis=-1, keepdims=True)) * factor)
            scale = 1.0 / jnp.sum(lifted, axis=-1, keepdims=True)
            attention.append((lifted * scale).astype(jnp.bfloat16))
        context_all = jnp.dot(
            jnp.concatenate(attention, axis=0), value, preferred_element_type=jnp.float32
        )
        context = context_all[:group_rows]
        for head in range(1, HEADS):
            context = jnp.where(
                lane_head == head, context_all[head * group_rows : (head + 1) * group_rows], context
            )
        result = before[at] + jnp.dot(
            context.astype(jnp.bfloat16), weights[5], preferred_element_type=jnp.float32
        )
        results.append(result.reshape(snaps, 1, SUBLANES, width))
    evolved = jnp.concatenate(results, axis=1).reshape(n_snap, snap_dev, vert_dev, width)

    low = lax.broadcasted_iota(jnp.int32, (n_snap * vert_dev, LANES), 1) < feat_width
    for at in range(0, n_feat, 2):
        lanes = slice(at * feat_width, (at + 2) * feat_width)
        first = evolved[:, 0, :, lanes].reshape(n_snap * vert_dev, LANES)
        second = evolved[:, 1, :, lanes].reshape(n_snap * vert_dev, LANES)
        even = jnp.where(low, first, pltpu.roll(second, feat_width, 1))
        odd = jnp.where(low, pltpu.roll(first, feat_width, 1), second)
        outgoing[at] = even.astype(jnp.bfloat16).reshape(n_snap, vert_dev, LANES)
        outgoing[at + 1] = odd.astype(jnp.bfloat16).reshape(n_snap, vert_dev, LANES)

    returns = []
    for step in sorted(range(1, total), key=lambda s: abs(2 * s - total)):
        peer = (me + step) % total
        copy = pltpu.make_async_remote_copy(
            src_ref=outgoing.at[peer % n_feat, peer // n_feat],
            dst_ref=returned.at[part, own],
            send_sem=return_send.at[step],
            recv_sem=return_recv.at[step],
            device_id=(peer // n_feat, peer % n_feat),
            device_id_type=MESH,
        )
        copy.start()
        returns.append(copy)
    own_copy = load(outgoing.at[me_feat, me_snap], returned.at[part, own], 0)
    for copy in gathers + sends:
        copy.wait_send()
    own_copy.wait()
    for copy in returns:
        copy.wait_recv()
    for copy in returns:
        copy.wait_send()


def on_device_fused(n_snap, n_feat, *operands):
    node_features, _, _, _, tile_values, layer_one = operands[:6]
    snap_dev, vert_count, feat_width = node_features.shape
    _, slot_total, tile_side, _ = tile_values.shape
    width = layer_one.shape[0]
    parts = n_feat // snap_dev
    snaps = n_snap * snap_dev
    vert_dev = vert_count // (parts * snaps)
    total = n_snap * n_feat
    kept = jnp.bfloat16
    result = pl.pallas_call(
        functools.partial(fused_kernel, n_snap, n_feat),
        out_shape=jax.ShapeDtypeStruct((parts, snaps, vert_dev, LANES), kept),
        in_specs=[pl.BlockSpec(memory_space=pltpu.HBM)] * 11,
        out_specs=pl.BlockSpec(memory_space=pl.ANY),
        scratch_shapes=[
            pltpu.VMEM((slot_total, tile_side, tile_side), kept),
            pltpu.VMEM((6, width, width), kept),
            pltpu.VMEM((n_feat, feat_width, vert_count), kept),
            pltpu.VMEM((vert_count, vert_count), kept),
            pltpu.VMEM((vert_count, width), kept),
            pltpu.VMEM((vert_count, width), kept),
            pltpu.VMEM((snaps, vert_dev, width), kept),
            pltpu.VMEM((snaps, vert_dev, width), kept),
            pltpu.VMEM((n_feat, n_snap, vert_dev, LANES), kept),
            pltpu.SemaphoreType.DMA((11,)),
            pltpu.SemaphoreType.DMA((n_feat,)),
            pltpu.SemaphoreType.DMA((n_feat,)),
            pltpu.SemaphoreType.DMA((snaps,)),
            pltpu.SemaphoreType.DMA((snaps,)),
            pltpu.SemaphoreType.DMA((total,)),
            pltpu.SemaphoreType.DMA((total,)),
            pltpu.SemaphoreType.REGULAR((n_snap // 4 + 1,)),
            pltpu.SMEM((snap_dev, slot_total), jnp.int32),
            pltpu.SMEM((snap_dev, slot_total), jnp.int32),
            pltpu.SMEM((snap_dev,), jnp.int32),
        ],
        compiler_params=pltpu.CompilerParams(collective_id=0, has_side_effects=True),
    )(*operands[1:4], node_features.transpose(0, 2, 1), *operands[4:])
    result = jnp.transpose(result.reshape(vert_count, LANES))
    return result.reshape(snap_dev, feat_width, vert_count).transpose(0, 2, 1)


def dispatch(n_snap, n_feat, *operands):
    snap_dev, vert_count, feat_width = operands[0].shape
    slot_total = operands[4].shape[1]
    snaps = n_snap * snap_dev
    fits = (
        snap_dev == 2
        and 2 * feat_width == LANES
        and n_feat % snap_dev == 0
        and n_feat % 2 == 0
        and n_snap >= 8
        and n_snap % 4 == 0
        and vert_count % (n_feat // snap_dev * snaps * 2 * SUBLANES) == 0
        and snaps * SUBLANES == LANES
        and slot_total <= 16
        and vert_count <= 1024
    )
    if fits:
        return on_device_fused(n_snap, n_feat, *operands)
    return on_device(*operands)


def solution(mesh):
    placed = (
        P("snap", None, "feat"),
        P("snap", None),
        P("snap", None),
        P("snap"),
        P("snap", None, None, None),
        P(),
        P(),
        P(),
        P(),
        P(),
        P(),
    )
    return jax.shard_map(
        functools.partial(dispatch, mesh.shape["snap"], mesh.shape["feat"]), mesh=mesh, in_specs=placed, out_specs=P("snap", None, "feat"), check_vma=False
    )
```

```python
import functools
import math

import jax
import jax.numpy as jnp
from jax import lax
from jax.experimental import pallas as pl
from jax.experimental.pallas import tpu as pltpu
from jax.sharding import PartitionSpec as P

HEADS = 8


masked_score = -1e30


def spread_padded(features, tile_block, block_rows, block_cols, slot_count):
    vert_count, feat_width = features.shape
    tile_side = tile_block.shape[1]
    slot_total = tile_block.shape[0]
    block_count = vert_count // tile_side
    blocked = features.reshape(block_count, tile_side, feat_width)
    picked_blocks = blocked[block_cols]
    live_slots = jnp.arange(slot_total, dtype=jnp.int32) < slot_count
    products = jnp.einsum(
        "irc,icf->irf", tile_block, picked_blocks, preferred_element_type=jnp.float32
    )
    products = products * live_slots.astype(jnp.float32)[:, None, None]
    membership = (
        (block_rows[None, :] == jnp.arange(block_count, dtype=jnp.int32)[:, None])
        & live_slots[None, :]
    ).astype(jnp.float32)
    summed = jnp.dot(
        membership,
        products.reshape(slot_total, tile_side * feat_width),
        precision=lax.Precision.HIGHEST,
    )
    return summed.reshape(vert_count, feat_width).astype(jnp.bfloat16)


def attend_local(hidden, query_weight, key_weight, value_weight, out_weight):
    snaps, verts, model_width = hidden.shape
    head_dim = model_width // HEADS
    flat = hidden.reshape(snaps * verts, model_width)

    def project(weight):
        return (
            jnp.dot(flat, weight, preferred_element_type=jnp.float32)
            .astype(jnp.bfloat16)
            .reshape(snaps, verts, HEADS, head_dim)
        )

    query_heads = project(query_weight)
    key_heads = project(key_weight)
    value_heads = project(value_weight)
    scores = jnp.einsum(
        "tvhd,uvhd->vhtu", query_heads, key_heads, preferred_element_type=jnp.float32
    ) * head_dim ** (-0.5)
    causal = (
        jnp.arange(snaps, dtype=jnp.int32)[:, None] >= jnp.arange(snaps, dtype=jnp.int32)[None, :]
    )
    scores = jnp.where(causal, scores, masked_score)
    row_max = jnp.max(scores, axis=-1, keepdims=True)
    lifted = jnp.exp(scores - row_max)
    weights = (lifted / jnp.sum(lifted, axis=-1, keepdims=True)).astype(jnp.bfloat16)
    context = jnp.einsum(
        "vhtu,uvhd->tvhd", weights, value_heads, preferred_element_type=jnp.float32
    ).astype(jnp.bfloat16)
    context = context.reshape(snaps * verts, model_width)
    result = flat.astype(jnp.float32) + jnp.dot(
        context, out_weight, preferred_element_type=jnp.float32
    )
    return result.astype(jnp.bfloat16).reshape(snaps, verts, model_width)


def on_device(
    node_features,
    tile_rows,
    tile_cols,
    tile_counts,
    tile_values,
    layer_one,
    layer_two,
    query_weight,
    key_weight,
    value_weight,
    out_weight,
):
    snap_dev, vert_count, feat_width = node_features.shape
    feat_index = lax.axis_index("feat")

    def spread_all(features):
        spread_pieces = []
        for snapshot in range(snap_dev):
            spread_pieces.append(
                spread_padded(
                    features[snapshot],
                    tile_values[snapshot],
                    tile_rows[snapshot],
                    tile_cols[snapshot],
                    tile_counts[snapshot],
                )
            )
        return jnp.stack(spread_pieces, axis=0)

    def convolve(features, weight):
        spread_rows = spread_all(features).reshape(snap_dev * vert_count, feat_width)
        own_columns = lax.dynamic_slice_in_dim(weight, feat_index * feat_width, feat_width, 1)
        mixed_sum = jnp.dot(
            lax.all_gather(spread_rows, "feat", axis=1, tiled=True),
            own_columns,
            preferred_element_type=jnp.float32,
        )
        mixed_sum = mixed_sum.reshape(snap_dev, vert_count, feat_width)
        return (features.astype(jnp.float32) + jnp.maximum(mixed_sum, 0.0)).astype(jnp.bfloat16)

    hidden_one = convolve(node_features, layer_one)
    hidden_two = convolve(hidden_one, layer_two)
    vertex_rows = lax.all_to_all(
        lax.all_to_all(hidden_two, "snap", split_axis=1, concat_axis=0, tiled=True),
        "feat",
        split_axis=1,
        concat_axis=2,
        tiled=True,
    )
    attended = attend_local(vertex_rows, query_weight, key_weight, value_weight, out_weight)
    return lax.all_to_all(
        lax.all_to_all(attended, "feat", split_axis=2, concat_axis=1, tiled=True),
        "snap",
        split_axis=0,
        concat_axis=1,
        tiled=True,
    )


LANES = 128
SUBLANES = 8
MESH = pl.DeviceIdType.MESH


def fused_kernel(
    n_snap,
    n_feat,
    rows_hbm,
    cols_hbm,
    counts_hbm,
    feat_ref,
    tiles_ref,
    w_one,
    w_two,
    w_query,
    w_key,
    w_value,
    w_out,
    returned,
    tiles,
    weights,
    pieces,
    adjacency,
    features,
    hidden_one,
    hidden_two,
    vertex_rows,
    outgoing,
    load_sem,
    gather_send,
    gather_recv,
    spread_send,
    spread_recv,
    return_send,
    return_recv,
    heard,
    rows_ref,
    cols_ref,
    counts_ref,
):
    snap_dev, feat_width, vert_count = feat_ref.shape
    slot_total, tile_side, _ = tiles.shape
    block_count = vert_count // tile_side
    snaps, vert_dev, width = vertex_rows.shape
    parts = n_feat // snap_dev
    part_rows = vert_count // parts
    total = n_snap * n_feat
    head_dim = width // HEADS

    me_snap = lax.axis_index("snap")
    me_feat = lax.axis_index("feat")
    me = me_snap * n_feat + me_feat
    part = me_feat % parts
    local = me_feat // parts
    own = me_snap * snap_dev + local

    def load(source, target, at):
        copy = pltpu.make_async_copy(source, target, load_sem.at[at])
        copy.start()
        return copy

    list_loads = [
        load(ref, kept, 8 + at)
        for at, (ref, kept) in enumerate(
            ((rows_hbm, rows_ref), (cols_hbm, cols_ref), (counts_hbm, counts_ref))
        )
    ]
    tile_load = load(tiles_ref.at[local], tiles, 1)
    weight_loads = [
        load(ref, weights.at[at], 2 + at)
        for at, ref in enumerate((w_one, w_two, w_query, w_key, w_value, w_out))
    ]

    barrier = pltpu.get_barrier_semaphore()
    twin = me_snap + 1 - 2 * (me_snap % 2)
    ring = [(me_snap + 2) % n_snap, (me_snap + n_snap - 2) % n_snap]
    mates = [(me_feat + step) % n_feat for step in range(1, n_feat)]

    def tell(semaphore, peers):
        for peer in peers:
            pl.semaphore_signal(semaphore, inc=1, device_id=peer, device_id_type=MESH)

    ring_peers = [(peer, me_feat) for peer in ring]
    twin_peer = [(twin, me_feat)]
    mate_peers = [(me_snap, mate) for mate in mates]
    tell(barrier, ring_peers + twin_peer + mate_peers)
    pl.semaphore_wait(barrier, len(ring_peers) + 1 + len(mate_peers))

    gathers = []
    for step in [n_feat // 2] + [s for s in range(1, n_feat) if s != n_feat // 2]:
        peer = (me_feat + step) % n_feat
        copy = pltpu.make_async_remote_copy(
            src_ref=feat_ref.at[peer // parts],
            dst_ref=pieces.at[me_feat],
            send_sem=gather_send.at[step],
            recv_sem=gather_recv.at[step],
            device_id=(me_snap, peer),
            device_id_type=MESH,
        )
        copy.start()
        gathers.append(copy)
    own_load = load(feat_ref.at[local], pieces.at[me_feat], 0)

    hops = n_snap // 4 - 1
    for hop in range(hops):
        tell(heard.at[hop], ring_peers)
        if hop + 1 < hops:
            pl.semaphore_wait(heard.at[hop], len(ring_peers))

    tile_load.wait()
    for copy in list_loads:
        copy.wait()
    slot_count = counts_ref[local]
    strip = 2 * SUBLANES
    places = []
    for slot in range(slot_total):
        place = rows_ref[local, slot] * block_count + cols_ref[local, slot]
        place = jnp.where(slot < slot_count, place, -1)
        places.append(jnp.full((strip, tile_side), place, jnp.int32))

    def build(at, carry):
        first = pl.multiple_of(at * strip, strip)
        listed = [
            tiles[slot, pl.ds(first, strip), :].astype(jnp.float32) for slot in range(slot_total)
        ]
        for row in range(block_count):
            for col in range(block_count):
                summed = jnp.zeros((strip, tile_side), jnp.float32)
                for slot in range(slot_total):
                    summed += jnp.where(
                        places[slot] == row * block_count + col, listed[slot], 0.0
                    )
                start = pl.multiple_of(row * tile_side + first, strip)
                adjacency[pl.ds(start, strip), col * tile_side : (col + 1) * tile_side] = (
                    summed.astype(jnp.bfloat16)
                )
        return carry

    strips = tile_side // strip
    lax.fori_loop(0, strips // 2, build, 0)
    pl.semaphore_wait(heard.at[hops - 1], len(ring_peers))
    tell(heard.at[hops], twin_peer)
    lax.fori_loop(strips // 2, strips, build, 0)
    pl.semaphore_wait(heard.at[hops], 1)
    tell(heard.at[hops + 1], mate_peers)

    for copy in weight_loads:
        copy.wait()
    for copy in gathers:
        copy.wait_recv()
    own_load.wait()
    features[...] = jnp.transpose(pieces[...].reshape(width, vert_count))

    def mix(lhs, source, before, weight):
        spread = jnp.dot(lhs, source, preferred_element_type=jnp.float32)
        mixed = jnp.dot(
            spread.astype(jnp.bfloat16), weight, preferred_element_type=jnp.float32
        )
        return (before.astype(jnp.float32) + jnp.maximum(mixed, 0.0)).astype(jnp.bfloat16)

    hidden_one[...] = mix(adjacency[...], features[...], features[...], weights[0])
    pl.semaphore_wait(heard.at[hops + 1], len(mate_peers))
    side = snaps // 2
    side_rows = side * vert_dev
    sends = []
    for turn in range(2):
        first = (own // side + 1 - turn) % 2 * side
        start = pl.multiple_of(part * part_rows + first * vert_dev, side_rows)
        own_rows = pl.ds(start, side_rows)
        hidden_two[pl.ds(first, side)] = mix(
            adjacency[own_rows, :], hidden_one[...], hidden_one[own_rows, :], weights[1]
        ).reshape(side, vert_dev, width)
        for step in range(turn, side):
            peer = first + (own % side + step) % side
            at = step + (1 - turn) * side
            copy = pltpu.make_async_remote_copy(
                src_ref=hidden_two.at[peer],
                dst_ref=vertex_rows.at[own],
                send_sem=spread_send.at[at],
                recv_sem=spread_recv.at[(own - peer + snaps) % snaps],
                device_id=(peer // snap_dev, (peer % snap_dev) * parts + part),
                device_id_type=MESH,
            )
            copy.start()
            sends.append(copy)
    vertex_rows[own] = hidden_two[own]
    for source in range(1, snaps):
        pltpu.make_async_copy(
            hidden_two.at[0], vertex_rows.at[0], spread_recv.at[source]
        ).wait()

    flat = vertex_rows[...].reshape(snaps * vert_dev, width)
    group_rows = snaps * SUBLANES
    groups = vert_dev // SUBLANES

    def split(array):
        array = array.reshape(snaps, groups, SUBLANES, width)
        return [array[:, at].reshape(group_rows, width) for at in range(groups)]

    def project(at):
        return split(jnp.dot(flat, weights[at], preferred_element_type=jnp.float32))

    queries, keys, values = project(2), project(3), project(4)
    before = split(flat.astype(jnp.float32))
    lane_head = lax.broadcasted_iota(jnp.int32, (group_rows, width), 1) // head_dim
    row_at = lax.broadcasted_iota(jnp.int32, (group_rows, group_rows), 0)
    col_at = lax.broadcasted_iota(jnp.int32, (group_rows, group_rows), 1)
    visible = (row_at % SUBLANES == col_at % SUBLANES) & (
        row_at // SUBLANES <= col_at // SUBLANES
    )
    factor = head_dim ** (-0.5) * math.log2(math.e)
    results = []
    for at in range(groups):
        query = queries[at].astype(jnp.bfloat16)
        value = jnp.transpose(values[at].astype(jnp.bfloat16))
        key = jnp.concatenate(
            [
                jnp.where(lane_head == head, keys[at], 0.0).astype(jnp.bfloat16)
                for head in range(HEADS)
            ],
            axis=0,
        )
        scores = lax.dot_general(
            key, query, (((1,), (1,)), ((), ())), preferred_element_type=jnp.float32
        )
        context = []
        for head in range(HEADS):
            score = scores[head * group_rows : (head + 1) * group_rows]
            score = jnp.where(visible, score, masked_score)
            lifted = jnp.exp2((score - jnp.max(score, axis=0, keepdims=True)) * factor)
            scale = 1.0 / jnp.sum(lifted, axis=0, keepdims=True)
            context.append(
                jnp.dot(
                    value[head * head_dim : (head + 1) * head_dim],
                    (lifted * scale).astype(jnp.bfloat16),
                    preferred_element_type=jnp.float32,
                )
            )
        context = jnp.transpose(jnp.concatenate(context, axis=0).astype(jnp.bfloat16))
        result = before[at] + jnp.dot(context, weights[5], preferred_element_type=jnp.float32)
        results.append(result.reshape(snaps, 1, SUBLANES, width))
    evolved = jnp.concatenate(results, axis=1).reshape(n_snap, snap_dev, vert_dev, width)

    low = lax.broadcasted_iota(jnp.int32, (n_snap * vert_dev, LANES), 1) < feat_width
    for at in range(0, n_feat, 2):
        lanes = slice(at * feat_width, (at + 2) * feat_width)
        first = evolved[:, 0, :, lanes].reshape(n_snap * vert_dev, LANES)
        second = evolved[:, 1, :, lanes].reshape(n_snap * vert_dev, LANES)
        even = jnp.where(low, first, pltpu.roll(second, feat_width, 1))
        odd = jnp.where(low, pltpu.roll(first, feat_width, 1), second)
        outgoing[at] = even.astype(jnp.bfloat16).reshape(n_snap, vert_dev, LANES)
        outgoing[at + 1] = odd.astype(jnp.bfloat16).reshape(n_snap, vert_dev, LANES)

    returns = []
    for step in sorted(range(1, total), key=lambda s: abs(2 * s - total)):
        peer = (me + step) % total
        copy = pltpu.make_async_remote_copy(
            src_ref=outgoing.at[peer % n_feat, peer // n_feat],
            dst_ref=returned.at[part, own],
            send_sem=return_send.at[step],
            recv_sem=return_recv.at[step],
            device_id=(peer // n_feat, peer % n_feat),
            device_id_type=MESH,
        )
        copy.start()
        returns.append(copy)
    own_copy = load(outgoing.at[me_feat, me_snap], returned.at[part, own], 0)
    for copy in gathers + sends:
        copy.wait_send()
    own_copy.wait()
    for copy in returns:
        copy.wait_recv()
    for copy in returns:
        copy.wait_send()


def on_device_fused(n_snap, n_feat, *operands):
    node_features, _, _, _, tile_values, layer_one = operands[:6]
    snap_dev, vert_count, feat_width = node_features.shape
    _, slot_total, tile_side, _ = tile_values.shape
    width = layer_one.shape[0]
    parts = n_feat // snap_dev
    snaps = n_snap * snap_dev
    vert_dev = vert_count // (parts * snaps)
    total = n_snap * n_feat
    kept = jnp.bfloat16
    result = pl.pallas_call(
        functools.partial(fused_kernel, n_snap, n_feat),
        out_shape=jax.ShapeDtypeStruct((parts, snaps, vert_dev, LANES), kept),
        in_specs=[pl.BlockSpec(memory_space=pltpu.HBM)] * 11,
        out_specs=pl.BlockSpec(memory_space=pl.ANY),
        scratch_shapes=[
            pltpu.VMEM((slot_total, tile_side, tile_side), kept),
            pltpu.VMEM((6, width, width), kept),
            pltpu.VMEM((n_feat, feat_width, vert_count), kept),
            pltpu.VMEM((vert_count, vert_count), kept),
            pltpu.VMEM((vert_count, width), kept),
            pltpu.VMEM((vert_count, width), kept),
            pltpu.VMEM((snaps, vert_dev, width), kept),
            pltpu.VMEM((snaps, vert_dev, width), kept),
            pltpu.VMEM((n_feat, n_snap, vert_dev, LANES), kept),
            pltpu.SemaphoreType.DMA((11,)),
            pltpu.SemaphoreType.DMA((n_feat,)),
            pltpu.SemaphoreType.DMA((n_feat,)),
            pltpu.SemaphoreType.DMA((snaps,)),
            pltpu.SemaphoreType.DMA((snaps,)),
            pltpu.SemaphoreType.DMA((total,)),
            pltpu.SemaphoreType.DMA((total,)),
            pltpu.SemaphoreType.REGULAR((n_snap // 4 + 1,)),
            pltpu.SMEM((snap_dev, slot_total), jnp.int32),
            pltpu.SMEM((snap_dev, slot_total), jnp.int32),
            pltpu.SMEM((snap_dev,), jnp.int32),
        ],
        compiler_params=pltpu.CompilerParams(collective_id=0, has_side_effects=True),
    )(*operands[1:4], node_features.transpose(0, 2, 1), *operands[4:])
    result = jnp.transpose(result.reshape(vert_count, LANES))
    return result.reshape(snap_dev, feat_width, vert_count).transpose(0, 2, 1)


def dispatch(n_snap, n_feat, *operands):
    snap_dev, vert_count, feat_width = operands[0].shape
    slot_total = operands[4].shape[1]
    snaps = n_snap * snap_dev
    fits = (
        snap_dev == 2
        and 2 * feat_width == LANES
        and n_feat % snap_dev == 0
        and n_feat % 2 == 0
        and n_snap >= 8
        and n_snap % 4 == 0
        and vert_count % (n_feat // snap_dev * snaps * 2 * SUBLANES) == 0
        and snaps * SUBLANES == LANES
        and slot_total <= 16
        and vert_count <= 1024
    )
    if fits:
        return on_device_fused(n_snap, n_feat, *operands)
    return on_device(*operands)


def solution(mesh):
    placed = (
        P("snap", None, "feat"),
        P("snap", None),
        P("snap", None),
        P("snap"),
        P("snap", None, None, None),
        P(),
        P(),
        P(),
        P(),
        P(),
        P(),
    )
    return jax.shard_map(
        functools.partial(dispatch, mesh.shape["snap"], mesh.shape["feat"]), mesh=mesh, in_specs=placed, out_specs=P("snap", None, "feat"), check_vma=False
    )
```

```python
import functools
import math

import jax
import jax.numpy as jnp
from jax import lax
from jax.experimental import pallas as pl
from jax.experimental.pallas import tpu as pltpu
from jax.sharding import PartitionSpec as P

HEADS = 8


masked_score = -1e30


def spread_padded(features, tile_block, block_rows, block_cols, slot_count):
    vert_count, feat_width = features.shape
    tile_side = tile_block.shape[1]
    slot_total = tile_block.shape[0]
    block_count = vert_count // tile_side
    blocked = features.reshape(block_count, tile_side, feat_width)
    picked_blocks = blocked[block_cols]
    live_slots = jnp.arange(slot_total, dtype=jnp.int32) < slot_count
    products = jnp.einsum(
        "irc,icf->irf", tile_block, picked_blocks, preferred_element_type=jnp.float32
    )
    products = products * live_slots.astype(jnp.float32)[:, None, None]
    membership = (
        (block_rows[None, :] == jnp.arange(block_count, dtype=jnp.int32)[:, None])
        & live_slots[None, :]
    ).astype(jnp.float32)
    summed = jnp.dot(
        membership,
        products.reshape(slot_total, tile_side * feat_width),
        precision=lax.Precision.HIGHEST,
    )
    return summed.reshape(vert_count, feat_width).astype(jnp.bfloat16)


def attend_local(hidden, query_weight, key_weight, value_weight, out_weight):
    snaps, verts, model_width = hidden.shape
    head_dim = model_width // HEADS
    flat = hidden.reshape(snaps * verts, model_width)

    def project(weight):
        return (
            jnp.dot(flat, weight, preferred_element_type=jnp.float32)
            .astype(jnp.bfloat16)
            .reshape(snaps, verts, HEADS, head_dim)
        )

    query_heads = project(query_weight)
    key_heads = project(key_weight)
    value_heads = project(value_weight)
    scores = jnp.einsum(
        "tvhd,uvhd->vhtu", query_heads, key_heads, preferred_element_type=jnp.float32
    ) * head_dim ** (-0.5)
    causal = (
        jnp.arange(snaps, dtype=jnp.int32)[:, None] >= jnp.arange(snaps, dtype=jnp.int32)[None, :]
    )
    scores = jnp.where(causal, scores, masked_score)
    row_max = jnp.max(scores, axis=-1, keepdims=True)
    lifted = jnp.exp(scores - row_max)
    weights = (lifted / jnp.sum(lifted, axis=-1, keepdims=True)).astype(jnp.bfloat16)
    context = jnp.einsum(
        "vhtu,uvhd->tvhd", weights, value_heads, preferred_element_type=jnp.float32
    ).astype(jnp.bfloat16)
    context = context.reshape(snaps * verts, model_width)
    result = flat.astype(jnp.float32) + jnp.dot(
        context, out_weight, preferred_element_type=jnp.float32
    )
    return result.astype(jnp.bfloat16).reshape(snaps, verts, model_width)


def on_device(
    node_features,
    tile_rows,
    tile_cols,
    tile_counts,
    tile_values,
    layer_one,
    layer_two,
    query_weight,
    key_weight,
    value_weight,
    out_weight,
):
    snap_dev, vert_count, feat_width = node_features.shape
    feat_index = lax.axis_index("feat")

    def spread_all(features):
        spread_pieces = []
        for snapshot in range(snap_dev):
            spread_pieces.append(
                spread_padded(
                    features[snapshot],
                    tile_values[snapshot],
                    tile_rows[snapshot],
                    tile_cols[snapshot],
                    tile_counts[snapshot],
                )
            )
        return jnp.stack(spread_pieces, axis=0)

    def convolve(features, weight):
        spread_rows = spread_all(features).reshape(snap_dev * vert_count, feat_width)
        own_columns = lax.dynamic_slice_in_dim(weight, feat_index * feat_width, feat_width, 1)
        mixed_sum = jnp.dot(
            lax.all_gather(spread_rows, "feat", axis=1, tiled=True),
            own_columns,
            preferred_element_type=jnp.float32,
        )
        mixed_sum = mixed_sum.reshape(snap_dev, vert_count, feat_width)
        return (features.astype(jnp.float32) + jnp.maximum(mixed_sum, 0.0)).astype(jnp.bfloat16)

    hidden_one = convolve(node_features, layer_one)
    hidden_two = convolve(hidden_one, layer_two)
    vertex_rows = lax.all_to_all(
        lax.all_to_all(hidden_two, "snap", split_axis=1, concat_axis=0, tiled=True),
        "feat",
        split_axis=1,
        concat_axis=2,
        tiled=True,
    )
    attended = attend_local(vertex_rows, query_weight, key_weight, value_weight, out_weight)
    return lax.all_to_all(
        lax.all_to_all(attended, "feat", split_axis=2, concat_axis=1, tiled=True),
        "snap",
        split_axis=0,
        concat_axis=1,
        tiled=True,
    )


LANES = 128
SUBLANES = 8
MESH = pl.DeviceIdType.MESH


def fused_kernel(
    n_snap,
    n_feat,
    rows_hbm,
    cols_hbm,
    counts_hbm,
    feat_ref,
    tiles_ref,
    w_one,
    w_two,
    w_query,
    w_key,
    w_value,
    w_out,
    returned,
    tiles,
    weights,
    pieces,
    adjacency,
    features,
    hidden_one,
    hidden_two,
    vertex_rows,
    outgoing,
    load_sem,
    gather_send,
    gather_recv,
    spread_send,
    spread_recv,
    return_send,
    return_recv,
    heard,
    rows_ref,
    cols_ref,
    counts_ref,
):
    snap_dev, feat_width, vert_count = feat_ref.shape
    slot_total, tile_side, _ = tiles.shape
    block_count = vert_count // tile_side
    snaps, vert_dev, width = vertex_rows.shape
    parts = n_feat // snap_dev
    part_rows = vert_count // parts
    total = n_snap * n_feat
    head_dim = width // HEADS

    me_snap = lax.axis_index("snap")
    me_feat = lax.axis_index("feat")
    me = me_snap * n_feat + me_feat
    part = me_feat % parts
    local = me_feat // parts
    own = me_snap * snap_dev + local

    def load(source, target, at):
        copy = pltpu.make_async_copy(source, target, load_sem.at[at])
        copy.start()
        return copy

    list_loads = [
        load(ref, kept, 8 + at)
        for at, (ref, kept) in enumerate(
            ((rows_hbm, rows_ref), (cols_hbm, cols_ref), (counts_hbm, counts_ref))
        )
    ]
    tile_load = load(tiles_ref.at[local], tiles, 1)
    weight_loads = [
        load(ref, weights.at[at], 2 + at)
        for at, ref in enumerate((w_one, w_two, w_query, w_key, w_value, w_out))
    ]

    barrier = pltpu.get_barrier_semaphore()
    twin = me_snap + 1 - 2 * (me_snap % 2)
    ring = [(me_snap + 2) % n_snap, (me_snap + n_snap - 2) % n_snap]
    mates = [(me_feat + step) % n_feat for step in range(1, n_feat)]

    def tell(semaphore, peers):
        for peer in peers:
            pl.semaphore_signal(semaphore, inc=1, device_id=peer, device_id_type=MESH)

    ring_peers = [(peer, me_feat) for peer in ring]
    twin_peer = [(twin, me_feat)]
    mate_peers = [(me_snap, mate) for mate in mates]
    tell(barrier, ring_peers + twin_peer + mate_peers)
    pl.semaphore_wait(barrier, len(ring_peers) + 1 + len(mate_peers))

    gathers = []
    for step in [n_feat // 2] + [s for s in range(1, n_feat) if s != n_feat // 2]:
        peer = (me_feat + step) % n_feat
        copy = pltpu.make_async_remote_copy(
            src_ref=feat_ref.at[peer // parts],
            dst_ref=pieces.at[me_feat],
            send_sem=gather_send.at[step],
            recv_sem=gather_recv.at[step],
            device_id=(me_snap, peer),
            device_id_type=MESH,
        )
        copy.start()
        gathers.append(copy)
    own_load = load(feat_ref.at[local], pieces.at[me_feat], 0)

    hops = n_snap // 4 - 1
    for hop in range(hops):
        tell(heard.at[hop], ring_peers)
        if hop + 1 < hops:
            pl.semaphore_wait(heard.at[hop], len(ring_peers))

    tile_load.wait()
    for copy in list_loads:
        copy.wait()
    slot_count = counts_ref[local]
    strip = 2 * SUBLANES
    places = []
    for slot in range(slot_total):
        place = rows_ref[local, slot] * block_count + cols_ref[local, slot]
        place = jnp.where(slot < slot_count, place, -1)
        places.append(jnp.full((strip, tile_side), place, jnp.int32))

    def build(at, carry):
        first = pl.multiple_of(at * strip, strip)
        listed = [
            tiles[slot, pl.ds(first, strip), :].astype(jnp.float32) for slot in range(slot_total)
        ]
        for row in range(block_count):
            for col in range(block_count):
                summed = jnp.zeros((strip, tile_side), jnp.float32)
                for slot in range(slot_total):
                    summed += jnp.where(
                        places[slot] == row * block_count + col, listed[slot], 0.0
                    )
                start = pl.multiple_of(row * tile_side + first, strip)
                adjacency[pl.ds(start, strip), col * tile_side : (col + 1) * tile_side] = (
                    summed.astype(jnp.bfloat16)
                )
        return carry

    strips = tile_side // strip
    lax.fori_loop(0, strips // 2, build, 0)
    pl.semaphore_wait(heard.at[hops - 1], len(ring_peers))
    tell(heard.at[hops], twin_peer)
    lax.fori_loop(strips // 2, strips, build, 0)
    pl.semaphore_wait(heard.at[hops], 1)
    tell(heard.at[hops + 1], mate_peers)

    for copy in weight_loads:
        copy.wait()
    for copy in gathers:
        copy.wait_recv()
    own_load.wait()
    features[...] = jnp.transpose(pieces[...].reshape(width, vert_count))

    def mix(lhs, source, before, weight):
        spread = jnp.dot(lhs, source, preferred_element_type=jnp.float32)
        mixed = jnp.dot(
            spread.astype(jnp.bfloat16), weight, preferred_element_type=jnp.float32
        )
        return (before.astype(jnp.float32) + jnp.maximum(mixed, 0.0)).astype(jnp.bfloat16)

    hidden_one[...] = mix(adjacency[...], features[...], features[...], weights[0])
    pl.semaphore_wait(heard.at[hops + 1], len(mate_peers))
    side = snaps // 2
    side_rows = side * vert_dev
    sends = []
    for turn in range(2):
        first = (own // side + 1 - turn) % 2 * side
        start = pl.multiple_of(part * part_rows + first * vert_dev, side_rows)
        own_rows = pl.ds(start, side_rows)
        hidden_two[pl.ds(first, side)] = mix(
            adjacency[own_rows, :], hidden_one[...], hidden_one[own_rows, :], weights[1]
        ).reshape(side, vert_dev, width)
        for step in range(turn, side):
            peer = first + (own % side + step) % side
            at = step + (1 - turn) * side
            copy = pltpu.make_async_remote_copy(
                src_ref=hidden_two.at[peer],
                dst_ref=vertex_rows.at[own],
                send_sem=spread_send.at[at],
                recv_sem=spread_recv.at[(own - peer + snaps) % snaps],
                device_id=(peer // snap_dev, (peer % snap_dev) * parts + part),
                device_id_type=MESH,
            )
            copy.start()
            sends.append(copy)
    vertex_rows[own] = hidden_two[own]
    for source in range(1, snaps):
        pltpu.make_async_copy(
            hidden_two.at[0], vertex_rows.at[0], spread_recv.at[source]
        ).wait()

    flat = vertex_rows[...].reshape(snaps * vert_dev, width)
    group_rows = snaps * SUBLANES
    groups = vert_dev // SUBLANES

    def split(array):
        array = array.reshape(snaps, groups, SUBLANES, width)
        return [array[:, at].reshape(group_rows, width) for at in range(groups)]

    def project(at):
        return split(jnp.dot(flat, weights[at], preferred_element_type=jnp.float32))

    queries, keys, values = project(2), project(3), project(4)
    before = split(flat.astype(jnp.float32))
    lane_head = lax.broadcasted_iota(jnp.int32, (group_rows, width), 1) // head_dim
    row_at = lax.broadcasted_iota(jnp.int32, (group_rows, group_rows), 0)
    col_at = lax.broadcasted_iota(jnp.int32, (group_rows, group_rows), 1)
    visible = (row_at % SUBLANES == col_at % SUBLANES) & (
        row_at // SUBLANES <= col_at // SUBLANES
    )
    factor = head_dim ** (-0.5) * math.log2(math.e)
    low = lax.broadcasted_iota(jnp.int32, (n_snap * SUBLANES, LANES), 1) < feat_width
    returns = []
    own_copies = []
    for at in range(groups):
        query = queries[at].astype(jnp.bfloat16)
        value = jnp.transpose(values[at].astype(jnp.bfloat16))
        key = jnp.concatenate(
            [
                jnp.where(lane_head == head, keys[at], 0.0).astype(jnp.bfloat16)
                for head in range(HEADS)
            ],
            axis=0,
        )
        scores = lax.dot_general(
            key, query, (((1,), (1,)), ((), ())), preferred_element_type=jnp.float32
        )
        context = []
        for head in range(HEADS):
            score = scores[head * group_rows : (head + 1) * group_rows]
            score = jnp.where(visible, score, masked_score)
            lifted = jnp.exp2((score - jnp.max(score, axis=0, keepdims=True)) * factor)
            scale = 1.0 / jnp.sum(lifted, axis=0, keepdims=True)
            context.append(
                jnp.dot(
                    value[head * head_dim : (head + 1) * head_dim],
                    (lifted * scale).astype(jnp.bfloat16),
                    preferred_element_type=jnp.float32,
                )
            )
        context = jnp.transpose(jnp.concatenate(context, axis=0).astype(jnp.bfloat16))
        result = before[at] + jnp.dot(context, weights[5], preferred_element_type=jnp.float32)
        evolved = result.reshape(n_snap, snap_dev, SUBLANES, width)
        for pair in range(0, n_feat, 2):
            lanes = slice(pair * feat_width, (pair + 2) * feat_width)
            early = evolved[:, 0, :, lanes].reshape(n_snap * SUBLANES, LANES)
            late = evolved[:, 1, :, lanes].reshape(n_snap * SUBLANES, LANES)
            even = jnp.where(low, early, pltpu.roll(late, feat_width, 1))
            odd = jnp.where(low, pltpu.roll(early, feat_width, 1), late)
            for other, lane_pair in ((pair, even), (pair + 1, odd)):
                outgoing[other, at] = lane_pair.astype(jnp.bfloat16).reshape(
                    n_snap, SUBLANES, LANES
                )
        for step in sorted(range(1, total), key=lambda s: abs(2 * s - total)):
            peer = (me + step) % total
            copy = pltpu.make_async_remote_copy(
                src_ref=outgoing.at[peer % n_feat, at, peer // n_feat],
                dst_ref=returned.at[part, own, at],
                send_sem=return_send.at[at, step],
                recv_sem=return_recv.at[at, step],
                device_id=(peer // n_feat, peer % n_feat),
                device_id_type=MESH,
            )
            copy.start()
            returns.append(copy)
        own_copies.append(
            load(outgoing.at[me_feat, at, me_snap], returned.at[part, own, at], at)
        )
    for copy in gathers + sends:
        copy.wait_send()
    for copy in own_copies:
        copy.wait()
    for copy in returns:
        copy.wait_recv()
    for copy in returns:
        copy.wait_send()


def on_device_fused(n_snap, n_feat, *operands):
    node_features, _, _, _, tile_values, layer_one = operands[:6]
    snap_dev, vert_count, feat_width = node_features.shape
    _, slot_total, tile_side, _ = tile_values.shape
    width = layer_one.shape[0]
    parts = n_feat // snap_dev
    snaps = n_snap * snap_dev
    vert_dev = vert_count // (parts * snaps)
    total = n_snap * n_feat
    kept = jnp.bfloat16
    result = pl.pallas_call(
        functools.partial(fused_kernel, n_snap, n_feat),
        out_shape=jax.ShapeDtypeStruct((parts, snaps, vert_dev // SUBLANES, SUBLANES, LANES), kept),
        in_specs=[pl.BlockSpec(memory_space=pltpu.HBM)] * 11,
        out_specs=pl.BlockSpec(memory_space=pl.ANY),
        scratch_shapes=[
            pltpu.VMEM((slot_total, tile_side, tile_side), kept),
            pltpu.VMEM((6, width, width), kept),
            pltpu.VMEM((n_feat, feat_width, vert_count), kept),
            pltpu.VMEM((vert_count, vert_count), kept),
            pltpu.VMEM((vert_count, width), kept),
            pltpu.VMEM((vert_count, width), kept),
            pltpu.VMEM((snaps, vert_dev, width), kept),
            pltpu.VMEM((snaps, vert_dev, width), kept),
            pltpu.VMEM((n_feat, vert_dev // SUBLANES, n_snap, SUBLANES, LANES), kept),
            pltpu.SemaphoreType.DMA((11,)),
            pltpu.SemaphoreType.DMA((n_feat,)),
            pltpu.SemaphoreType.DMA((n_feat,)),
            pltpu.SemaphoreType.DMA((snaps,)),
            pltpu.SemaphoreType.DMA((snaps,)),
            pltpu.SemaphoreType.DMA((vert_dev // SUBLANES, total)),
            pltpu.SemaphoreType.DMA((vert_dev // SUBLANES, total)),
            pltpu.SemaphoreType.REGULAR((n_snap // 4 + 1,)),
            pltpu.SMEM((snap_dev, slot_total), jnp.int32),
            pltpu.SMEM((snap_dev, slot_total), jnp.int32),
            pltpu.SMEM((snap_dev,), jnp.int32),
        ],
        compiler_params=pltpu.CompilerParams(collective_id=0, has_side_effects=True),
    )(*operands[1:4], node_features.transpose(0, 2, 1), *operands[4:])
    result = jnp.transpose(result.reshape(vert_count, LANES))
    return result.reshape(snap_dev, feat_width, vert_count).transpose(0, 2, 1)


def dispatch(n_snap, n_feat, *operands):
    snap_dev, vert_count, feat_width = operands[0].shape
    slot_total = operands[4].shape[1]
    snaps = n_snap * snap_dev
    fits = (
        snap_dev == 2
        and 2 * feat_width == LANES
        and n_feat % snap_dev == 0
        and n_feat % 2 == 0
        and n_snap >= 8
        and n_snap % 4 == 0
        and vert_count % (n_feat // snap_dev * snaps * 2 * SUBLANES) == 0
        and snaps * SUBLANES == LANES
        and slot_total <= 16
        and vert_count <= 1024
    )
    if fits:
        return on_device_fused(n_snap, n_feat, *operands)
    return on_device(*operands)


def solution(mesh):
    placed = (
        P("snap", None, "feat"),
        P("snap", None),
        P("snap", None),
        P("snap"),
        P("snap", None, None, None),
        P(),
        P(),
        P(),
        P(),
        P(),
        P(),
    )
    return jax.shard_map(
        functools.partial(dispatch, mesh.shape["snap"], mesh.shape["feat"]), mesh=mesh, in_specs=placed, out_specs=P("snap", None, "feat"), check_vma=False
    )
```
